32 devices in a mesh: cfg: 2 (over x), seq: 8 (over z, y), head: 2 (over core).
Axes of the slice: x: 2, y: 2, z: 4, core: 2. Of those that a mesh axis runs over, the one named last changes fastest.
Arguments:
- queries: bfloat16 [2, 640, 1536], P('cfg', 'seq', 'head'), may hold values from -8 to 8
- keys: bfloat16 [2, 640, 1536], P('cfg', 'seq', 'head'), may hold values from -8 to 8
- values: bfloat16 [2, 640, 1536], P('cfg', 'seq', 'head'), may hold values from -6 to 6
- w_out: bfloat16 [1536, 64], P('head'), may hold values from -1.1953125 to 1.1953125
- latents: float32 [640, 64], P('seq', 'cfg'), may hold values from -6 to 6
- block_mask: int32 [8, 8], replicated, may hold values from 0 to 1, as said below
- lengths: int32 [8], replicated, may hold values from 20 to 80, as said below
- step_index: int32 [1], replicated, may hold values from 0 to 49
Outputs:
- denoised: float32 [640, 64], P('seq', 'cfg')
- stepped: float32 [640, 64], P('seq', 'cfg')
The draws below stay inside these ranges and needn't reach their ends.
Inputs may be any that keep to these rules, and one draw needn't show every extreme that they name: `block_mask`: every diagonal entry is 1. `lengths`: some shard is full in every draw.
All inputs are finite; a program needn't handle non-finite values.
Results may differ from the reference program's by a relative error of at most 0.0055.
Values may be sent and summed in bfloat16 or wider, within the bound.
A program may use at most 64 MiB of HBM per device.

```python
import jax
import jax.numpy as jnp
from jax import lax

HEADS = 24
HEAD_DIM = 64
LATENT = 64
STEPS = 50
TOK_DEV = 80
SHARDS = 8
TOKENS = 640
HEAD_COLS = 1536


def paired_draw(key):
    base = jax.random.fold_in(key, 11)
    shape = (2, TOKENS, HEAD_COLS)
    query_draw = jnp.clip(jax.random.normal(jax.random.fold_in(base, 1), shape, jnp.float32), -6.0, 6.0)
    key_draw = jnp.clip(jax.random.normal(jax.random.fold_in(base, 2), shape, jnp.float32), -6.0, 6.0)
    return (query_draw, key_draw)


def draw_queries(key, part):
    return paired_draw(key)[0].astype(jnp.bfloat16)


def draw_keys(key, part):
    return paired_draw(key)[1].astype(jnp.bfloat16)


def draw_block_mask(key, part):
    level = jax.random.randint(jax.random.fold_in(key, 21), (SHARDS, 1), 1, 4)
    rolled = jax.random.randint(jax.random.fold_in(key, 22), (SHARDS, SHARDS), 0, 4)
    marked = (rolled < level).astype(jnp.int32)
    diagonal = (jnp.arange(SHARDS)[:, None] == jnp.arange(SHARDS)[None, :]).astype(jnp.int32)
    return jnp.maximum(marked, diagonal)


def draw_lengths(key, part):
    counts = jax.random.randint(jax.random.fold_in(key, 31), (SHARDS,), TOK_DEV // 4, TOK_DEV + 1)
    chosen = jax.random.randint(jax.random.fold_in(key, 32), (), 0, SHARDS)
    return jnp.where(jnp.arange(SHARDS) == chosen, TOK_DEV, counts).astype(jnp.int32)


def block_scale(key, shape, split, low, high):
    gain, own = 1.0, jax.random.fold_in(key, 6)
    for dim, parts in split:
        steps = jnp.exp(jax.random.uniform(jax.random.fold_in(own, dim), (parts,), jnp.float32, low / len(split), high / len(split)))
        gain = gain * jnp.repeat(steps, shape[dim] // parts).reshape([-1 if axis == dim else 1 for axis in range(len(shape))])
    return gain


def centred(key, extent, scale, bound, shards=(), dtype=jnp.bfloat16):
    values = scale * jax.random.normal(key, extent, jnp.float32)
    if shards:
        values = values * block_scale(key, extent, shards, -0.22, 0.18)
    return jnp.clip(values, -bound, bound).astype(dtype)


def setup_inputs(seed: int = 0) -> dict:
    key_of = jax.random.split(jax.random.key(seed), 9)
    return {
        "queries": draw_queries(jax.random.fold_in(key_of[8], 71), 0),
        "keys": draw_keys(jax.random.fold_in(key_of[8], 71), 0),
        "values": centred(key_of[2], (2, TOKENS, HEAD_COLS), 1.0, 6.0, ((0, 2), (1, 8), (2, 2))),
        "w_out": centred(key_of[3], (HEAD_COLS, LATENT), 0.2, 1.1953125, ((0, 2),)),
        "latents": centred(key_of[4], (TOKENS, LATENT), 1.0, 6.0, ((0, 8), (1, 2)), jnp.float32),
        "block_mask": draw_block_mask(jax.random.fold_in(key_of[8], 71), 0),
        "lengths": draw_lengths(jax.random.fold_in(key_of[8], 71), 0),
        "step_index": jax.random.randint(key_of[7], (1,), 0, STEPS).astype(jnp.int32),
    }


guide_scale = 6.0

def plan(step_value):
    step_float = step_value.astype(jnp.float32)
    first = (STEPS - step_float + 1.0) / (STEPS + 1.0)
    second = (STEPS - step_float) / (STEPS + 1.0)
    abar_now = jnp.exp(-6.0 * first * first)
    abar_next = jnp.exp(-6.0 * second * second)
    return (jnp.sqrt(abar_now), jnp.sqrt(1.0 - abar_now), jnp.sqrt(abar_next), jnp.sqrt(1.0 - abar_next))

def reference(queries, keys, values, w_out, latents, block_mask, lengths, step_index):
    slot_valid = jnp.arange(TOKENS) % TOK_DEV < jnp.repeat(lengths, TOK_DEV)
    mask_rows = block_mask.reshape(SHARDS, SHARDS)

    def half_prediction(half):
        key_all = keys[half].astype(jnp.float32).reshape(TOKENS, HEADS, HEAD_DIM)
        value_all = values[half].astype(jnp.float32).reshape(TOKENS, HEADS, HEAD_DIM)
        query_blocks = queries[half].astype(jnp.float32).reshape(SHARDS, TOK_DEV, HEADS, HEAD_DIM)

        def one_shard(pair):
            query_block, mask_row = pair
            allowed = (jnp.repeat(mask_row, TOK_DEV) > 0) & slot_valid
            scores = jnp.einsum('qhd,khd->hqk', query_block, key_all) * 0.125
            scores = jnp.where(allowed[None, None, :], scores, -1e+30)
            rowmax = lax.optimization_barrier(jnp.max(scores, axis=-1, keepdims=True))
            weights = jnp.where(allowed[None, None, :], jnp.exp(scores - rowmax), 0.0)
            total = lax.optimization_barrier(jnp.sum(weights, axis=-1))
            rounded = weights.astype(jnp.bfloat16).astype(jnp.float32)
            summed = jnp.einsum('hqk,khd->hqd', rounded, value_all)
            attended = summed / total[..., None]
            return jnp.transpose(attended, (1, 0, 2)).reshape(TOK_DEV, HEAD_COLS).astype(jnp.bfloat16)
        attended = lax.map(one_shard, (query_blocks, mask_rows)).reshape(TOKENS, HEAD_COLS)
        return jnp.dot(attended, w_out, preferred_element_type=jnp.float32)
    conditional = half_prediction(0)
    unconditional = half_prediction(1)
    guided = unconditional + guide_scale * (conditional - unconditional)
    coef_a, coef_b, coef_a2, coef_b2 = plan(step_index[0])
    denoised = coef_a * latents - coef_b * guided
    stepped = coef_a2 * denoised + coef_b2 * (coef_b * latents + coef_a * guided)
    return (denoised, stepped)
```

```python
import jax
import jax.numpy as jnp
from jax import lax
from jax.experimental import pallas as pl
from jax.experimental.pallas import tpu as pltpu
from jax.sharding import PartitionSpec as P

HEAD_DIM = 64
STEPS = 50


guide_scale = 6.0
score_scale = 0.125


def from_partner(value, axis, distance):
    mask = 2**distance
    pairs = [(source, source ^ mask) for source in range(lax.axis_size(axis))]
    return lax.ppermute(value, axis, pairs)


def shifted(block, axis, distance):
    devices = range(lax.axis_size(axis))
    route = [((i - distance) % len(devices), i) for i in devices]
    return lax.ppermute(block, axis, route)


def plan(step_value):
    step_float = step_value.astype(jnp.float32)
    first = (STEPS - step_float + 1.0) / (STEPS + 1.0)
    second = (STEPS - step_float) / (STEPS + 1.0)
    abar_now = jnp.exp(-6.0 * first * first)
    abar_next = jnp.exp(-6.0 * second * second)
    return (
        jnp.sqrt(abar_now),
        jnp.sqrt(1.0 - abar_now),
        jnp.sqrt(abar_next),
        jnp.sqrt(1.0 - abar_next),
    )


def regroup_heads(triple, bit, own_shard):
    upper = jnp.right_shift(own_shard, bit) % 2 == 1
    kept = []
    sent = []
    for member in triple:
        width = member.shape[1] // 2
        lower_cols = member[:, :width]
        upper_cols = member[:, width:]
        kept.append(jnp.where(upper, upper_cols, lower_cols))
        sent.append(jnp.where(upper, lower_cols, upper_cols))
    arrived = from_partner((sent[0], sent[1], sent[2]), "seq", bit)
    joined = []
    for mine, theirs in zip(kept, arrived):
        joined.append(
            jnp.where(upper, jnp.concatenate([theirs, mine], 0), jnp.concatenate([mine, theirs], 0))
        )
    return (joined[0], joined[1], joined[2])


def regroup_tokens(member, bit, own_shard):
    upper = jnp.right_shift(own_shard, bit) % 2 == 1
    height = member.shape[0] // 2
    lower_rows = member[:height]
    upper_rows = member[height:]
    kept = jnp.where(upper, upper_rows, lower_rows)
    sent = jnp.where(upper, lower_rows, upper_rows)
    arrived = from_partner(sent, "seq", bit)
    return jnp.where(
        upper, jnp.concatenate([arrived, kept], 1), jnp.concatenate([kept, arrived], 1)
    )


def local(queries, keys, values, w_out, latents, block_mask, lengths, step_index):
    row_count, columns = queries[0].shape
    shard_total = lax.axis_size("seq")
    levels = 1
    group = 2**levels
    own_shard = lax.axis_index("seq")
    triple = (queries[0], keys[0], values[0])
    bit = 0
    triple = regroup_heads(triple, bit, own_shard)
    query_group, key_group, value_group = triple
    group_rows = group * row_count
    group_cols = columns // group
    head_count = group_cols // HEAD_DIM
    group_index = own_shard // group
    group_count = shard_total // group
    query_heads = query_group.reshape(group_rows, head_count, HEAD_DIM)
    slot_offsets = jnp.arange(row_count)
    initial = (
        jnp.full((head_count, group_rows), -1e30, jnp.float32),
        jnp.zeros((head_count, group_rows), jnp.float32),
        jnp.zeros((head_count, group_rows, HEAD_DIM), jnp.float32),
    )

    def absorb(carry, piece, owner):
        key_piece, value_piece = piece
        submask = lax.dynamic_slice(
            block_mask, (group_index * group, owner * group), (group, group)
        )
        live_counts = lax.dynamic_slice_in_dim(lengths, owner * group, group)
        key_valid = (slot_offsets[None, :] < live_counts[:, None]).reshape(group_rows)
        pair_mask = jnp.repeat(jnp.repeat(submask > 0, row_count, axis=0), row_count, axis=1)
        keep = pair_mask & key_valid[None, :]

        def attend(state):
            running, total, accum = state
            scores = (
                jnp.einsum(
                    "qhd,khd->hqk",
                    query_heads,
                    key_piece.reshape(group_rows, head_count, HEAD_DIM),
                    preferred_element_type=jnp.float32,
                )
                * score_scale
            )
            scores = jnp.where(keep[None], scores, -1e30)
            newmax = jnp.maximum(running, jnp.max(scores, axis=-1))
            weights = jnp.where(keep[None], jnp.exp(scores - newmax[..., None]), 0.0)
            factor = jnp.exp(running - newmax)
            total = total * factor + jnp.sum(weights, axis=-1)
            accum = accum * factor[..., None] + jnp.einsum(
                "hqk,khd->hqd",
                weights.astype(jnp.bfloat16),
                value_piece.reshape(group_rows, head_count, HEAD_DIM),
                preferred_element_type=jnp.float32,
            )
            return (newmax, total, accum)

        return lax.cond(jnp.any(submask > 0), attend, lambda state: state, carry)

    carry = absorb(initial, (key_group, value_group), group_index)

    def one_turn(turn_index, state):
        held, totals = state
        held = shifted((held[0], held[1]), "seq", group)
        owner_index = (group_index - turn_index) % group_count
        totals = absorb(totals, held, owner_index)
        return (held, totals)

    held_last, carry = lax.fori_loop(1, group_count, one_turn, ((key_group, value_group), carry))
    running, total, accum = carry
    attended = (
        jnp.transpose(accum / total[..., None], (1, 0, 2))
        .reshape(group_rows, group_cols)
        .astype(jnp.bfloat16)
    )
    for bit in reversed(range(levels)):
        attended = regroup_tokens(attended, bit, own_shard)
    partial_value = jnp.dot(attended, w_out, preferred_element_type=jnp.float32)
    half_index = lax.axis_index("cfg")
    own_width = latents.shape[1]
    own_start = half_index * own_width
    prediction = lax.psum(partial_value, "head")
    mine = lax.dynamic_slice_in_dim(prediction, own_start, own_width, 1)
    outgoing = lax.dynamic_slice_in_dim(prediction, (1 - half_index) * own_width, own_width, 1)
    other_half = from_partner(outgoing, "cfg", 0)
    conditional = jnp.where(half_index == 0, mine, other_half)
    unconditional = jnp.where(half_index == 0, other_half, mine)
    guided = unconditional + guide_scale * (conditional - unconditional)
    coef_a, coef_b, coef_a2, coef_b2 = plan(step_index[0])
    denoised = coef_a * latents - coef_b * guided
    stepped = coef_a2 * denoised + coef_b2 * (coef_b * latents + coef_a * guided)
    return (denoised, stepped)


PAIR = 2 * HEAD_DIM
NEG = -1e30
LOG2E = 1.4426950408889634
ORDER = (4, 0, 1, 2, 3, 5)
RETURN = jnp.bfloat16
BATCHES = ((0, 1), (1, 3), (4, 4))


def owner_of(pair, head):
    if pair < 4:
        return pair + 2
    return head if pair == 4 else 7 - head


def joint_kernel(
    q_hbm, k_hbm, v_hbm, w_hbm, mask_hbm, len_hbm,
    out_ref,
    qbuf, kbuf, vbuf, abuf, arecv, wbuf, bias, part,
    send_sem, recv_sem, own_sem, w_sem, ret_send, ret_recv, x_send, x_recv,
    here, cross_here, sibling_here,
    part_sem, mask_ref, len_ref, small_sem,
):
    cfg = lax.axis_index("cfg")
    me = lax.axis_index("seq")
    head = lax.axis_index("head")
    rows = q_hbm.shape[0]
    half = me // 4
    mesh = pl.DeviceIdType.MESH
    sources = (k_hbm, v_hbm, q_hbm)
    buffers = (kbuf, vbuf, qbuf)

    def slot(kind, shard):
        return buffers[kind].at[pl.ds(pl.multiple_of(shard * rows, 16), rows)]

    def columns(kind, pair):
        return sources[kind].at[:, pl.ds(pl.multiple_of(pair * PAIR, PAIR), PAIR)]

    def remote(kind, pair, target):
        return pltpu.make_async_remote_copy(
            src_ref=columns(kind, pair),
            dst_ref=slot(kind, me),
            send_sem=send_sem.at[kind, pair],
            recv_sem=recv_sem.at[kind, me],
            device_id={"seq": target},
            device_id_type=mesh,
        )

    def arrival(kind, shard):
        return pltpu.make_async_remote_copy(
            src_ref=slot(kind, shard),
            dst_ref=slot(kind, shard),
            send_sem=send_sem.at[kind, 0],
            recv_sem=recv_sem.at[kind, shard],
            device_id={"seq": shard},
            device_id_type=mesh,
        )

    def own_copy(kind, pair):
        return pltpu.make_async_copy(columns(kind, pair), slot(kind, me), own_sem.at[kind])

    width = part.shape[0]

    def channels(half_index):
        return pl.ds(pl.multiple_of(half_index * width, 16), width)

    def returned(target, source, pair, shard, index):
        return pltpu.make_async_remote_copy(
            src_ref=abuf.at[index, channels(target)],
            dst_ref=arecv.at[source, pair],
            send_sem=ret_send.at[target, index],
            recv_sem=ret_recv.at[source, pair],
            device_id={"cfg": target, "seq": shard},
            device_id_type=mesh,
        )

    inner = (me >= 2) & (me < 6)
    low = me == head
    high = me == 7 - head
    active = inner | low | high
    my_pair = jnp.where(inner, me - 2, jnp.where(low, 4, 5))

    barrier = pltpu.get_barrier_semaphore()
    for other in range(1, 8):

        @pl.when(other > me)
        def _(other=other):
            pl.semaphore_signal(barrier, inc=1, device_id={"seq": other}, device_id_type=mesh)

    @pl.when(head == 0)
    def _():
        pl.semaphore_signal(barrier, inc=1, device_id={"head": 1}, device_id_type=mesh)

    w_copy = pltpu.make_async_copy(w_hbm, wbuf, w_sem)
    small_copies = [
        pltpu.make_async_copy(mask_hbm, mask_ref, small_sem.at[0]),
        pltpu.make_async_copy(len_hbm, len_ref, small_sem.at[1]),
    ]

    greeted = me + cfg + head

    @pl.when(greeted > 0)
    def _():
        pl.semaphore_wait(barrier, greeted)

    @pl.when(cfg == 0)
    def _():
        pl.semaphore_signal(barrier, inc=1, device_id={"cfg": 1}, device_id_type=mesh)

    for other in range(7):

        @pl.when(other < me)
        def _(other=other):
            pl.semaphore_signal(here.at[me], inc=1, device_id={"seq": other}, device_id_type=mesh)

    @pl.when(head == 1)
    def _():
        pl.semaphore_signal(sibling_here, inc=1, device_id={"head": 0}, device_id_type=mesh)

    @pl.when(active)
    def _():
        for kind in range(3):
            own_copy(kind, my_pair).start()

    for copy in small_copies:
        copy.start()
    w_copy.start()

    def await_shard(shard):
        @pl.when(shard > me)
        def _():
            pl.semaphore_wait(here.at[shard], 1)

    def send(kind, place):
        pair = ORDER[place]
        target = owner_of(pair, head)

        @pl.when(target != me)
        def _():
            remote(kind, pair, target).start()

    await_shard(1)
    for place in range(3):
        if place:
            await_shard(place + 1)
        send(0, place)
        send(1, place)

        @pl.when(half == 0)
        def _(place=place):
            send(2, place)

    for place in range(3, 6):
        await_shard(place + 1)
        if place == 5:
            await_shard(7)
        send(0, place)
        send(1, place)

    @pl.when(cfg == 1)
    def _():
        pl.semaphore_signal(cross_here, inc=1, device_id={"cfg": 0}, device_id_type=mesh)

    @pl.when(half == 1)
    def _():
        for place in range(3):
            send(2, place)

    for place in range(3, 6):
        send(2, place)

    for copy in small_copies:
        copy.wait()
    @pl.when(active)
    def _():
        lane = lax.broadcasted_iota(jnp.int32, (8, 8 * rows), 1)
        row_shard = lax.broadcasted_iota(jnp.int32, (8, 8 * rows), 0)
        position = lane % rows
        limit = jnp.zeros((8, 8 * rows), jnp.int32)
        for j in range(8):
            column = jnp.zeros((8, 8 * rows), jnp.int32)
            for i in range(8):
                live = jnp.where(mask_ref[i, j] > 0, len_ref[j], 0)
                column = jnp.where(row_shard == i, live, column)
            limit = jnp.where((lane >= j * rows) & (lane < (j + 1) * rows), column, limit)
        bias[...] = jnp.where(position < limit, 0.0, NEG).reshape(8, 1, 8 * rows)

        w_copy.wait()
        weight = wbuf[:, pl.ds(pl.multiple_of(my_pair * PAIR, PAIR), PAIR)]

        for kind in range(2):
            own_copy(kind, my_pair).wait()
            for step in range(1, 8):
                shard = ((half + step // 4) % 2) * 4 + (me % 4 + step) % 4
                arrival(kind, shard).wait_recv()

        def attend(first, count):
            height = count * rows
            query = qbuf[pl.ds(pl.multiple_of(first * rows, 16), height)]
            zero = jnp.zeros_like(query)
            left = lax.broadcasted_iota(jnp.int32, (height, PAIR), 1) < HEAD_DIM
            stacked = jnp.concatenate(
                [jnp.where(left, query, zero), jnp.where(left, zero, query)], axis=0
            )
            scores = lax.dot_general(
                stacked, kbuf[...], (((1,), (1,)), ((), ())), preferred_element_type=jnp.float32
            )
            shape = scores.shape
            scores = scores.reshape(2, count, rows, 8 * rows) + bias[pl.ds(first, count)][None]
            scores = scores.reshape(shape)
            top = jnp.max(scores, axis=1, keepdims=True)
            weights = jnp.exp2((scores - top) * (score_scale * LOG2E))
            total = jnp.sum(weights, axis=1, keepdims=True)
            summed = jnp.dot(
                weights.astype(jnp.bfloat16), vbuf[...], preferred_element_type=jnp.float32
            )
            summed = summed / total
            attended = jnp.where(left, summed[:height], summed[height:]).astype(jnp.bfloat16)
            for index in range(count):
                abuf[first + index] = lax.dot_general(
                    weight,
                    attended[index * rows : (index + 1) * rows],
                    (((1,), (1,)), ((), ())),
                    preferred_element_type=jnp.float32,
                ).astype(RETURN)

        def give(shard):
            @pl.when(shard != me)
            def _():
                returned(cfg, cfg, my_pair, shard, shard).start()

            returned(1 - cfg, cfg, my_pair, shard, shard).start()

        @pl.when(cfg == 0)
        def _():
            pl.semaphore_wait(cross_here, 1)

        own_copy(2, my_pair).wait()

        def await_query(shard):
            @pl.when(shard != me)
            def _():
                arrival(2, shard).wait_recv()

        for first, count in BATCHES:
            for shard in range(first, first + count):
                await_query(shard)
            attend(first, count)
            for shard in range(first, first + count):
                give(shard)
        arecv[cfg, my_pair] = abuf[me, channels(cfg)]

    @pl.when(jnp.logical_not(active))
    def _():
        w_copy.wait()

        @pl.when(cfg == 0)
        def _():
            pl.semaphore_wait(cross_here, 1)

    @pl.when(head == 0)
    def _():
        pl.semaphore_wait(sibling_here, 1)

    for source in range(2):
        for pair in range(6):

            @pl.when((owner_of(pair, head) != me) | (cfg != source))
            def _(source=source, pair=pair):
                returned(1 - cfg, source, pair, 0, 0).wait_recv()

    def summed_pairs(source):
        parts = [arecv[source, pair].astype(jnp.float32) for pair in range(6)]
        return ((parts[0] + parts[1]) + (parts[2] + parts[3])) + (parts[4] + parts[5])

    conditional = summed_pairs(0)
    unconditional = summed_pairs(1)
    part[...] = unconditional + guide_scale * (conditional - unconditional)
    sibling = pltpu.make_async_remote_copy(
        src_ref=part,
        dst_ref=out_ref.at[head],
        send_sem=x_send,
        recv_sem=x_recv,
        device_id={"head": 1 - head},
        device_id_type=mesh,
    )
    sibling.start()
    own_part = pltpu.make_async_copy(part, out_ref.at[head], part_sem)
    own_part.start()

    for kind in range(3):
        for place in range(6):
            pair = ORDER[place]
            target = owner_of(pair, head)

            @pl.when(target != me)
            def _(kind=kind, pair=pair, target=target):
                remote(kind, pair, target).wait_send()

    @pl.when(active)
    def _():
        for step in range(8):
            shard = (me + step) % 8
            if step:
                returned(cfg, cfg, my_pair, shard, shard).wait_send()
            returned(1 - cfg, cfg, my_pair, shard, shard).wait_send()

    pltpu.make_async_remote_copy(
        src_ref=part,
        dst_ref=out_ref.at[1 - head],
        send_sem=x_send,
        recv_sem=x_recv,
        device_id={"head": 1 - head},
        device_id_type=mesh,
    ).wait_recv()
    sibling.wait_send()
    own_part.wait()


def joint(queries, keys, values, w_out, latents, block_mask, lengths, step_index):
    rows, cols = queries.shape[1:]
    hbm = pl.BlockSpec(memory_space=pltpu.HBM)
    dma = pltpu.SemaphoreType.DMA
    regular = pltpu.SemaphoreType.REGULAR
    width = latents.shape[1]
    latent = w_out.shape[1]
    small = jnp.int32
    packed = pl.pallas_call(
        joint_kernel,
        out_shape=jax.ShapeDtypeStruct((2, width, rows), jnp.float32),
        in_specs=[hbm] * 6,
        out_specs=hbm,
        scratch_shapes=[
            pltpu.VMEM((8 * rows, PAIR), jnp.bfloat16),
            pltpu.VMEM((8 * rows, PAIR), jnp.bfloat16),
            pltpu.VMEM((8 * rows, PAIR), jnp.bfloat16),
            pltpu.VMEM((8, latent, rows), RETURN),
            pltpu.VMEM((2, 6, width, rows), RETURN),
            pltpu.VMEM((latent, cols), jnp.bfloat16),
            pltpu.VMEM((8, 1, 8 * rows), jnp.float32),
            pltpu.VMEM((width, rows), jnp.float32),
            dma((3, 6)),
            dma((3, 8)),
            dma((3,)),
            dma,
            dma((2, 8)),
            dma((2, 6)),
            dma,
            dma,
            regular((8,)),
            regular,
            regular,
            dma,
            pltpu.SMEM(block_mask.shape, small),
            pltpu.SMEM(lengths.shape, small),
            dma((2,)),
        ],
        compiler_params=pltpu.CompilerParams(collective_id=0, has_side_effects=True),
    )(queries[0], keys[0], values[0], w_out.T, block_mask, lengths)
    guided = packed[0] + packed[1]
    tokens = latents.T
    coef_a, coef_b, coef_a2, coef_b2 = plan(jnp.where(guided == guided, step_index[0], 0))
    denoised = coef_a * tokens - coef_b * guided
    stepped = coef_a2 * denoised + coef_b2 * (coef_b * tokens + coef_a * guided)
    return (denoised.T, stepped.T)


def solution(mesh):
    in_specs = (
        P("cfg", "seq", "head"),
        P("cfg", "seq", "head"),
        P("cfg", "seq", "head"),
        P("head", None),
        P("seq", "cfg"),
        P(),
        P(),
        P(),
    )
    out_specs = (P("seq", "cfg"), P("seq", "cfg"))
    sizes = mesh.shape
    fits = sizes["cfg"] == 2 and sizes["seq"] == 8 and sizes["head"] == 2
    body = joint if fits else local
    return jax.shard_map(body, mesh=mesh, in_specs=in_specs, out_specs=out_specs, check_vma=False)
```

```python
import jax
import jax.numpy as jnp
from jax import lax
from jax.experimental import pallas as pl
from jax.experimental.pallas import tpu as pltpu
from jax.sharding import PartitionSpec as P

HEAD_DIM = 64
STEPS = 50


guide_scale = 6.0
score_scale = 0.125


def from_partner(value, axis, distance):
    mask = 2**distance
    pairs = [(source, source ^ mask) for source in range(lax.axis_size(axis))]
    return lax.ppermute(value, axis, pairs)


def shifted(block, axis, distance):
    devices = range(lax.axis_size(axis))
    route = [((i - distance) % len(devices), i) for i in devices]
    return lax.ppermute(block, axis, route)


def plan(step_value):
    step_float = step_value.astype(jnp.float32)
    first = (STEPS - step_float + 1.0) / (STEPS + 1.0)
    second = (STEPS - step_float) / (STEPS + 1.0)
    abar_now = jnp.exp(-6.0 * first * first)
    abar_next = jnp.exp(-6.0 * second * second)
    return (
        jnp.sqrt(abar_now),
        jnp.sqrt(1.0 - abar_now),
        jnp.sqrt(abar_next),
        jnp.sqrt(1.0 - abar_next),
    )


def regroup_heads(triple, bit, own_shard):
    upper = jnp.right_shift(own_shard, bit) % 2 == 1
    kept = []
    sent = []
    for member in triple:
        width = member.shape[1] // 2
        lower_cols = member[:, :width]
        upper_cols = member[:, width:]
        kept.append(jnp.where(upper, upper_cols, lower_cols))
        sent.append(jnp.where(upper, lower_cols, upper_cols))
    arrived = from_partner((sent[0], sent[1], sent[2]), "seq", bit)
    joined = []
    for mine, theirs in zip(kept, arrived):
        joined.append(
            jnp.where(upper, jnp.concatenate([theirs, mine], 0), jnp.concatenate([mine, theirs], 0))
        )
    return (joined[0], joined[1], joined[2])


def regroup_tokens(member, bit, own_shard):
    upper = jnp.right_shift(own_shard, bit) % 2 == 1
    height = member.shape[0] // 2
    lower_rows = member[:height]
    upper_rows = member[height:]
    kept = jnp.where(upper, upper_rows, lower_rows)
    sent = jnp.where(upper, lower_rows, upper_rows)
    arrived = from_partner(sent, "seq", bit)
    return jnp.where(
        upper, jnp.concatenate([arrived, kept], 1), jnp.concatenate([kept, arrived], 1)
    )


def local(queries, keys, values, w_out, latents, block_mask, lengths, step_index):
    row_count, columns = queries[0].shape
    shard_total = lax.axis_size("seq")
    levels = 1
    group = 2**levels
    own_shard = lax.axis_index("seq")
    triple = (queries[0], keys[0], values[0])
    bit = 0
    triple = regroup_heads(triple, bit, own_shard)
    query_group, key_group, value_group = triple
    group_rows = group * row_count
    group_cols = columns // group
    head_count = group_cols // HEAD_DIM
    group_index = own_shard // group
    group_count = shard_total // group
    query_heads = query_group.reshape(group_rows, head_count, HEAD_DIM)
    slot_offsets = jnp.arange(row_count)
    initial = (
        jnp.full((head_count, group_rows), -1e30, jnp.float32),
        jnp.zeros((head_count, group_rows), jnp.float32),
        jnp.zeros((head_count, group_rows, HEAD_DIM), jnp.float32),
    )

    def absorb(carry, piece, owner):
        key_piece, value_piece = piece
        submask = lax.dynamic_slice(
            block_mask, (group_index * group, owner * group), (group, group)
        )
        live_counts = lax.dynamic_slice_in_dim(lengths, owner * group, group)
        key_valid = (slot_offsets[None, :] < live_counts[:, None]).reshape(group_rows)
        pair_mask = jnp.repeat(jnp.repeat(submask > 0, row_count, axis=0), row_count, axis=1)
        keep = pair_mask & key_valid[None, :]

        def attend(state):
            running, total, accum = state
            scores = (
                jnp.einsum(
                    "qhd,khd->hqk",
                    query_heads,
                    key_piece.reshape(group_rows, head_count, HEAD_DIM),
                    preferred_element_type=jnp.float32,
                )
                * score_scale
            )
            scores = jnp.where(keep[None], scores, -1e30)
            newmax = jnp.maximum(running, jnp.max(scores, axis=-1))
            weights = jnp.where(keep[None], jnp.exp(scores - newmax[..., None]), 0.0)
            factor = jnp.exp(running - newmax)
            total = total * factor + jnp.sum(weights, axis=-1)
            accum = accum * factor[..., None] + jnp.einsum(
                "hqk,khd->hqd",
                weights.astype(jnp.bfloat16),
                value_piece.reshape(group_rows, head_count, HEAD_DIM),
                preferred_element_type=jnp.float32,
            )
            return (newmax, total, accum)

        return lax.cond(jnp.any(submask > 0), attend, lambda state: state, carry)

    carry = absorb(initial, (key_group, value_group), group_index)

    def one_turn(turn_index, state):
        held, totals = state
        held = shifted((held[0], held[1]), "seq", group)
        owner_index = (group_index - turn_index) % group_count
        totals = absorb(totals, held, owner_index)
        return (held, totals)

    held_last, carry = lax.fori_loop(1, group_count, one_turn, ((key_group, value_group), carry))
    running, total, accum = carry
    attended = (
        jnp.transpose(accum / total[..., None], (1, 0, 2))
        .reshape(group_rows, group_cols)
        .astype(jnp.bfloat16)
    )
    for bit in reversed(range(levels)):
        attended = regroup_tokens(attended, bit, own_shard)
    partial_value = jnp.dot(attended, w_out, preferred_element_type=jnp.float32)
    half_index = lax.axis_index("cfg")
    own_width = latents.shape[1]
    own_start = half_index * own_width
    prediction = lax.psum(partial_value, "head")
    mine = lax.dynamic_slice_in_dim(prediction, own_start, own_width, 1)
    outgoing = lax.dynamic_slice_in_dim(prediction, (1 - half_index) * own_width, own_width, 1)
    other_half = from_partner(outgoing, "cfg", 0)
    conditional = jnp.where(half_index == 0, mine, other_half)
    unconditional = jnp.where(half_index == 0, other_half, mine)
    guided = unconditional + guide_scale * (conditional - unconditional)
    coef_a, coef_b, coef_a2, coef_b2 = plan(step_index[0])
    denoised = coef_a * latents - coef_b * guided
    stepped = coef_a2 * denoised + coef_b2 * (coef_b * latents + coef_a * guided)
    return (denoised, stepped)


PAIR = 2 * HEAD_DIM
NEG = -1e30
LOG2E = 1.4426950408889634
ORDER = (4, 0, 1, 2, 3, 5)
RETURN = jnp.bfloat16
BATCHES = ((0, 1), (1, 3), (4, 4))


def owner_of(pair, head):
    if pair < 4:
        return pair + 2
    return head if pair == 4 else 1 + 5 * head


def joint_kernel(
    q_hbm, k_hbm, v_hbm, w_hbm, mask_hbm, len_hbm,
    out_ref,
    qbuf, kbuf, vbuf, abuf, arecv, wbuf, bias, part,
    send_sem, recv_sem, own_sem, w_sem, ret_send, ret_recv, x_send, x_recv,
    here, cross_here, sibling_here,
    part_sem, mask_ref, len_ref, small_sem,
):
    cfg = lax.axis_index("cfg")
    me = lax.axis_index("seq")
    head = lax.axis_index("head")
    rows = q_hbm.shape[0]
    half = me // 4
    mesh = pl.DeviceIdType.MESH
    sources = (k_hbm, v_hbm, q_hbm)
    buffers = (kbuf, vbuf, qbuf)

    def slot(kind, shard):
        return buffers[kind].at[pl.ds(pl.multiple_of(shard * rows, 16), rows)]

    def columns(kind, pair):
        return sources[kind].at[:, pl.ds(pl.multiple_of(pair * PAIR, PAIR), PAIR)]

    def remote(kind, pair, target):
        return pltpu.make_async_remote_copy(
            src_ref=columns(kind, pair),
            dst_ref=slot(kind, me),
            send_sem=send_sem.at[kind, pair],
            recv_sem=recv_sem.at[kind, me],
            device_id={"seq": target},
            device_id_type=mesh,
        )

    def arrival(kind, shard):
        return pltpu.make_async_remote_copy(
            src_ref=slot(kind, shard),
            dst_ref=slot(kind, shard),
            send_sem=send_sem.at[kind, 0],
            recv_sem=recv_sem.at[kind, shard],
            device_id={"seq": shard},
            device_id_type=mesh,
        )

    def own_copy(kind, pair):
        return pltpu.make_async_copy(columns(kind, pair), slot(kind, me), own_sem.at[kind])

    width = part.shape[0]

    def channels(half_index):
        return pl.ds(pl.multiple_of(half_index * width, 16), width)

    def returned(target, source, pair, shard, index):
        return pltpu.make_async_remote_copy(
            src_ref=abuf.at[index, channels(target)],
            dst_ref=arecv.at[source, pair],
            send_sem=ret_send.at[target, index],
            recv_sem=ret_recv.at[source, pair],
            device_id={"cfg": target, "seq": shard},
            device_id_type=mesh,
        )

    inner = (me >= 2) & (me < 6)
    low = me == head
    high = me == owner_of(5, head)
    active = inner | low | high
    my_pair = jnp.where(inner, me - 2, jnp.where(low, 4, 5))

    barrier = pltpu.get_barrier_semaphore()
    for other in range(1, 8):

        @pl.when(other > me)
        def _(other=other):
            pl.semaphore_signal(barrier, inc=1, device_id={"seq": other}, device_id_type=mesh)

    @pl.when(head == 0)
    def _():
        pl.semaphore_signal(barrier, inc=1, device_id={"head": 1}, device_id_type=mesh)

    w_copy = pltpu.make_async_copy(w_hbm, wbuf, w_sem)
    small_copies = [
        pltpu.make_async_copy(mask_hbm, mask_ref, small_sem.at[0]),
        pltpu.make_async_copy(len_hbm, len_ref, small_sem.at[1]),
    ]

    greeted = me + cfg + head

    @pl.when(greeted > 0)
    def _():
        pl.semaphore_wait(barrier, greeted)

    @pl.when(cfg == 0)
    def _():
        pl.semaphore_signal(barrier, inc=1, device_id={"cfg": 1}, device_id_type=mesh)

    for other in range(7):

        @pl.when(other < me)
        def _(other=other):
            pl.semaphore_signal(here.at[me], inc=1, device_id={"seq": other}, device_id_type=mesh)

    @pl.when(head == 1)
    def _():
        pl.semaphore_signal(sibling_here, inc=1, device_id={"head": 0}, device_id_type=mesh)

    @pl.when(active)
    def _():
        for kind in range(3):
            own_copy(kind, my_pair).start()

    for copy in small_copies:
        copy.start()
    w_copy.start()

    def await_shard(shard):
        @pl.when(shard > me)
        def _():
            pl.semaphore_wait(here.at[shard], 1)

    def send(kind, place):
        pair = ORDER[place]
        target = owner_of(pair, head)

        @pl.when(target != me)
        def _():
            remote(kind, pair, target).start()

    await_shard(1)
    send(0, 0)
    send(1, 0)

    @pl.when(head == 0)
    def _():
        send(0, 5)
        send(1, 5)

    for place in range(1, 3):
        await_shard(place + 1)
        send(0, place)
        send(1, place)

    @pl.when(half == 1)
    def _():
        for place in range(3):
            send(2, place)

        @pl.when(head == 0)
        def _():
            send(2, 5)

    for place in range(3, 5):
        await_shard(place + 1)
        send(0, place)
        send(1, place)
    await_shard(6)

    @pl.when(jnp.logical_not(head == 0))
    def _():
        send(0, 5)
        send(1, 5)

    @pl.when(half == 0)
    def _():
        for place in range(3):
            send(2, place)

    for place in range(3, 5):
        send(2, place)

    @pl.when((half == 0) | (head == 1))
    def _():
        send(2, 5)

    await_shard(7)

    @pl.when(cfg == 1)
    def _():
        pl.semaphore_signal(cross_here, inc=1, device_id={"cfg": 0}, device_id_type=mesh)


    for copy in small_copies:
        copy.wait()
    @pl.when(active)
    def _():
        lane = lax.broadcasted_iota(jnp.int32, (8, 8 * rows), 1)
        row_shard = lax.broadcasted_iota(jnp.int32, (8, 8 * rows), 0)
        position = lane % rows
        limit = jnp.zeros((8, 8 * rows), jnp.int32)
        for j in range(8):
            column = jnp.zeros((8, 8 * rows), jnp.int32)
            for i in range(8):
                live = jnp.where(mask_ref[i, j] > 0, len_ref[j], 0)
                column = jnp.where(row_shard == i, live, column)
            limit = jnp.where((lane >= j * rows) & (lane < (j + 1) * rows), column, limit)
        bias[...] = jnp.where(position < limit, 0.0, NEG).reshape(8, 1, 8 * rows)

        w_copy.wait()
        weight = wbuf[:, pl.ds(pl.multiple_of(my_pair * PAIR, PAIR), PAIR)]

        for kind in range(2):
            own_copy(kind, my_pair).wait()
            for step in range(1, 8):
                shard = ((half + step // 4) % 2) * 4 + (me % 4 + step) % 4
                arrival(kind, shard).wait_recv()

        def attend(first, count):
            height = count * rows
            query = qbuf[pl.ds(pl.multiple_of(first * rows, 16), height)]
            zero = jnp.zeros_like(query)
            left = lax.broadcasted_iota(jnp.int32, (height, PAIR), 1) < HEAD_DIM
            stacked = jnp.concatenate(
                [jnp.where(left, query, zero), jnp.where(left, zero, query)], axis=0
            )
            scores = lax.dot_general(
                stacked, kbuf[...], (((1,), (1,)), ((), ())), preferred_element_type=jnp.float32
            )
            shape = scores.shape
            scores = scores.reshape(2, count, rows, 8 * rows) + bias[pl.ds(first, count)][None]
            scores = scores.reshape(shape)
            top = jnp.max(scores, axis=1, keepdims=True)
            weights = jnp.exp2((scores - top) * (score_scale * LOG2E))
            total = jnp.sum(weights, axis=1, keepdims=True)
            summed = jnp.dot(
                weights.astype(jnp.bfloat16), vbuf[...], preferred_element_type=jnp.float32
            )
            summed = summed / total
            attended = jnp.where(left, summed[:height], summed[height:]).astype(jnp.bfloat16)
            for index in range(count):
                abuf[first + index] = lax.dot_general(
                    weight,
                    attended[index * rows : (index + 1) * rows],
                    (((1,), (1,)), ((), ())),
                    preferred_element_type=jnp.float32,
                ).astype(RETURN)

        def give(shard):
            @pl.when(shard != me)
            def _():
                returned(cfg, cfg, my_pair, shard, shard).start()

            returned(1 - cfg, cfg, my_pair, shard, shard).start()

        @pl.when(cfg == 0)
        def _():
            pl.semaphore_wait(cross_here, 1)

        own_copy(2, my_pair).wait()

        def await_query(shard):
            @pl.when(shard != me)
            def _():
                arrival(2, shard).wait_recv()

        def batch(first, count):
            for shard in range(first, first + count):
                await_query(shard)
            attend(first, count)
            for shard in range(first, first + count):
                give(shard)

        batch(0, 1)

        @pl.when(half == 0)
        def _():
            batch(1, 3)
            batch(6, 2)
            batch(4, 2)

        @pl.when(half == 1)
        def _():
            batch(4, 4)
            batch(1, 3)

        arecv[cfg, my_pair] = abuf[me, channels(cfg)]

    @pl.when(jnp.logical_not(active))
    def _():
        w_copy.wait()

        @pl.when(cfg == 0)
        def _():
            pl.semaphore_wait(cross_here, 1)

    @pl.when(head == 0)
    def _():
        pl.semaphore_wait(sibling_here, 1)

    for source in range(2):
        for pair in range(6):

            @pl.when((owner_of(pair, head) != me) | (cfg != source))
            def _(source=source, pair=pair):
                returned(1 - cfg, source, pair, 0, 0).wait_recv()

    def summed_pairs(source):
        parts = [arecv[source, pair].astype(jnp.float32) for pair in range(6)]
        return ((parts[0] + parts[1]) + (parts[2] + parts[3])) + (parts[4] + parts[5])

    conditional = summed_pairs(0)
    unconditional = summed_pairs(1)
    part[...] = unconditional + guide_scale * (conditional - unconditional)
    sibling = pltpu.make_async_remote_copy(
        src_ref=part,
        dst_ref=out_ref.at[head],
        send_sem=x_send,
        recv_sem=x_recv,
        device_id={"head": 1 - head},
        device_id_type=mesh,
    )
    sibling.start()
    own_part = pltpu.make_async_copy(part, out_ref.at[head], part_sem)
    own_part.start()

    for kind in range(3):
        for place in range(6):
            pair = ORDER[place]
            target = owner_of(pair, head)

            @pl.when(target != me)
            def _(kind=kind, pair=pair, target=target):
                remote(kind, pair, target).wait_send()

    @pl.when(active)
    def _():
        for step in range(8):
            shard = (me + step) % 8
            if step:
                returned(cfg, cfg, my_pair, shard, shard).wait_send()
            returned(1 - cfg, cfg, my_pair, shard, shard).wait_send()

    pltpu.make_async_remote_copy(
        src_ref=part,
        dst_ref=out_ref.at[1 - head],
        send_sem=x_send,
        recv_sem=x_recv,
        device_id={"head": 1 - head},
        device_id_type=mesh,
    ).wait_recv()
    sibling.wait_send()
    own_part.wait()


def joint(queries, keys, values, w_out, latents, block_mask, lengths, step_index):
    rows, cols = queries.shape[1:]
    hbm = pl.BlockSpec(memory_space=pltpu.HBM)
    dma = pltpu.SemaphoreType.DMA
    regular = pltpu.SemaphoreType.REGULAR
    width = latents.shape[1]
    latent = w_out.shape[1]
    small = jnp.int32
    packed = pl.pallas_call(
        joint_kernel,
        out_shape=jax.ShapeDtypeStruct((2, width, rows), jnp.float32),
        in_specs=[hbm] * 6,
        out_specs=pl.BlockSpec(memory_space=pl.ANY),
        scratch_shapes=[
            pltpu.VMEM((8 * rows, PAIR), jnp.bfloat16),
            pltpu.VMEM((8 * rows, PAIR), jnp.bfloat16),
            pltpu.VMEM((8 * rows, PAIR), jnp.bfloat16),
            pltpu.VMEM((8, latent, rows), RETURN),
            pltpu.VMEM((2, 6, width, rows), RETURN),
            pltpu.VMEM((latent, cols), jnp.bfloat16),
            pltpu.VMEM((8, 1, 8 * rows), jnp.float32),
            pltpu.VMEM((width, rows), jnp.float32),
            dma((3, 6)),
            dma((3, 8)),
            dma((3,)),
            dma,
            dma((2, 8)),
            dma((2, 6)),
            dma,
            dma,
            regular((8,)),
            regular,
            regular,
            dma,
            pltpu.SMEM(block_mask.shape, small),
            pltpu.SMEM(lengths.shape, small),
            dma((2,)),
        ],
        compiler_params=pltpu.CompilerParams(collective_id=0, has_side_effects=True, vmem_limit_bytes=6 * 1024 * 1024),
    )(*[pltpu.with_memory_space_constraint(x, pltpu.HBM) for x in (queries[0], keys[0], values[0], w_out.T, block_mask, lengths)])
    guided = packed[0] + packed[1]
    tokens = latents.T
    coef_a, coef_b, coef_a2, coef_b2 = plan(jnp.where(guided == guided, step_index[0], 0))
    denoised = coef_a * tokens - coef_b * guided
    stepped = coef_a2 * denoised + coef_b2 * (coef_b * tokens + coef_a * guided)
    return (denoised.T, stepped.T)


def solution(mesh):
    in_specs = (
        P("cfg", "seq", "head"),
        P("cfg", "seq", "head"),
        P("cfg", "seq", "head"),
        P("head", None),
        P("seq", "cfg"),
        P(),
        P(),
        P(),
    )
    out_specs = (P("seq", "cfg"), P("seq", "cfg"))
    sizes = mesh.shape
    fits = sizes["cfg"] == 2 and sizes["seq"] == 8 and sizes["head"] == 2
    body = joint if fits else local
    return jax.shard_map(body, mesh=mesh, in_specs=in_specs, out_specs=out_specs, check_vma=False)
```

```python
import jax
import jax.numpy as jnp
from jax import lax
from jax.experimental import pallas as pl
from jax.experimental.pallas import tpu as pltpu
from jax.sharding import PartitionSpec as P

HEAD_DIM = 64
STEPS = 50


guide_scale = 6.0
score_scale = 0.125


def from_partner(value, axis, distance):
    mask = 2**distance
    pairs = [(source, source ^ mask) for source in range(lax.axis_size(axis))]
    return lax.ppermute(value, axis, pairs)


def shifted(block, axis, distance):
    devices = range(lax.axis_size(axis))
    route = [((i - distance) % len(devices), i) for i in devices]
    return lax.ppermute(block, axis, route)


def plan(step_value):
    step_float = step_value.astype(jnp.float32)
    first = (STEPS - step_float + 1.0) / (STEPS + 1.0)
    second = (STEPS - step_float) / (STEPS + 1.0)
    abar_now = jnp.exp(-6.0 * first * first)
    abar_next = jnp.exp(-6.0 * second * second)
    return (
        jnp.sqrt(abar_now),
        jnp.sqrt(1.0 - abar_now),
        jnp.sqrt(abar_next),
        jnp.sqrt(1.0 - abar_next),
    )


def regroup_heads(triple, bit, own_shard):
    upper = jnp.right_shift(own_shard, bit) % 2 == 1
    kept = []
    sent = []
    for member in triple:
        width = member.shape[1] // 2
        lower_cols = member[:, :width]
        upper_cols = member[:, width:]
        kept.append(jnp.where(upper, upper_cols, lower_cols))
        sent.append(jnp.where(upper, lower_cols, upper_cols))
    arrived = from_partner((sent[0], sent[1], sent[2]), "seq", bit)
    joined = []
    for mine, theirs in zip(kept, arrived):
        joined.append(
            jnp.where(upper, jnp.concatenate([theirs, mine], 0), jnp.concatenate([mine, theirs], 0))
        )
    return (joined[0], joined[1], joined[2])


def regroup_tokens(member, bit, own_shard):
    upper = jnp.right_shift(own_shard, bit) % 2 == 1
    height = member.shape[0] // 2
    lower_rows = member[:height]
    upper_rows = member[height:]
    kept = jnp.where(upper, upper_rows, lower_rows)
    sent = jnp.where(upper, lower_rows, upper_rows)
    arrived = from_partner(sent, "seq", bit)
    return jnp.where(
        upper, jnp.concatenate([arrived, kept], 1), jnp.concatenate([kept, arrived], 1)
    )


def local(queries, keys, values, w_out, latents, block_mask, lengths, step_index):
    row_count, columns = queries[0].shape
    shard_total = lax.axis_size("seq")
    levels = 1
    group = 2**levels
    own_shard = lax.axis_index("seq")
    triple = (queries[0], keys[0], values[0])
    bit = 0
    triple = regroup_heads(triple, bit, own_shard)
    query_group, key_group, value_group = triple
    group_rows = group * row_count
    group_cols = columns // group
    head_count = group_cols // HEAD_DIM
    group_index = own_shard // group
    group_count = shard_total // group
    query_heads = query_group.reshape(group_rows, head_count, HEAD_DIM)
    slot_offsets = jnp.arange(row_count)
    initial = (
        jnp.full((head_count, group_rows), -1e30, jnp.float32),
        jnp.zeros((head_count, group_rows), jnp.float32),
        jnp.zeros((head_count, group_rows, HEAD_DIM), jnp.float32),
    )

    def absorb(carry, piece, owner):
        key_piece, value_piece = piece
        submask = lax.dynamic_slice(
            block_mask, (group_index * group, owner * group), (group, group)
        )
        live_counts = lax.dynamic_slice_in_dim(lengths, owner * group, group)
        key_valid = (slot_offsets[None, :] < live_counts[:, None]).reshape(group_rows)
        pair_mask = jnp.repeat(jnp.repeat(submask > 0, row_count, axis=0), row_count, axis=1)
        keep = pair_mask & key_valid[None, :]

        def attend(state):
            running, total, accum = state
            scores = (
                jnp.einsum(
                    "qhd,khd->hqk",
                    query_heads,
                    key_piece.reshape(group_rows, head_count, HEAD_DIM),
                    preferred_element_type=jnp.float32,
                )
                * score_scale
            )
            scores = jnp.where(keep[None], scores, -1e30)
            newmax = jnp.maximum(running, jnp.max(scores, axis=-1))
            weights = jnp.where(keep[None], jnp.exp(scores - newmax[..., None]), 0.0)
            factor = jnp.exp(running - newmax)
            total = total * factor + jnp.sum(weights, axis=-1)
            accum = accum * factor[..., None] + jnp.einsum(
                "hqk,khd->hqd",
                weights.astype(jnp.bfloat16),
                value_piece.reshape(group_rows, head_count, HEAD_DIM),
                preferred_element_type=jnp.float32,
            )
            return (newmax, total, accum)

        return lax.cond(jnp.any(submask > 0), attend, lambda state: state, carry)

    carry = absorb(initial, (key_group, value_group), group_index)

    def one_turn(turn_index, state):
        held, totals = state
        held = shifted((held[0], held[1]), "seq", group)
        owner_index = (group_index - turn_index) % group_count
        totals = absorb(totals, held, owner_index)
        return (held, totals)

    held_last, carry = lax.fori_loop(1, group_count, one_turn, ((key_group, value_group), carry))
    running, total, accum = carry
    attended = (
        jnp.transpose(accum / total[..., None], (1, 0, 2))
        .reshape(group_rows, group_cols)
        .astype(jnp.bfloat16)
    )
    for bit in reversed(range(levels)):
        attended = regroup_tokens(attended, bit, own_shard)
    partial_value = jnp.dot(attended, w_out, preferred_element_type=jnp.float32)
    half_index = lax.axis_index("cfg")
    own_width = latents.shape[1]
    own_start = half_index * own_width
    prediction = lax.psum(partial_value, "head")
    mine = lax.dynamic_slice_in_dim(prediction, own_start, own_width, 1)
    outgoing = lax.dynamic_slice_in_dim(prediction, (1 - half_index) * own_width, own_width, 1)
    other_half = from_partner(outgoing, "cfg", 0)
    conditional = jnp.where(half_index == 0, mine, other_half)
    unconditional = jnp.where(half_index == 0, other_half, mine)
    guided = unconditional + guide_scale * (conditional - unconditional)
    coef_a, coef_b, coef_a2, coef_b2 = plan(step_index[0])
    denoised = coef_a * latents - coef_b * guided
    stepped = coef_a2 * denoised + coef_b2 * (coef_b * latents + coef_a * guided)
    return (denoised, stepped)


PAIR = 2 * HEAD_DIM
NEG = -1e30
LOG2E = 1.4426950408889634
ORDER = (4, 0, 1, 2, 3, 5)
RETURN = jnp.bfloat16
BATCHES = ((0, 1), (1, 3), (4, 4))


def owner_of(pair, head):
    if pair < 4:
        return pair + 2
    return head if pair == 4 else 1 + 5 * head


def joint_kernel(
    q_hbm, k_hbm, v_hbm, w_hbm, mask_hbm, len_hbm,
    out_ref,
    qbuf, kbuf, vbuf, abuf, arecv, wbuf, bias, part,
    send_sem, recv_sem, own_sem, w_sem, ret_send, ret_recv,
    here, cross_ready, pair_ready,
    part_sem, mask_ref, len_ref, small_sem,
):
    cfg = lax.axis_index("cfg")
    me = lax.axis_index("seq")
    head = lax.axis_index("head")
    rows = q_hbm.shape[0]
    half = me // 4
    mesh = pl.DeviceIdType.MESH
    sources = (k_hbm, v_hbm, q_hbm)
    buffers = (kbuf, vbuf, qbuf)

    def slot(kind, shard):
        return buffers[kind].at[pl.ds(pl.multiple_of(shard * rows, 16), rows)]

    def columns(kind, pair):
        return sources[kind].at[:, pl.ds(pl.multiple_of(pair * PAIR, PAIR), PAIR)]

    def remote(kind, pair, target):
        return pltpu.make_async_remote_copy(
            src_ref=columns(kind, pair),
            dst_ref=slot(kind, me),
            send_sem=send_sem.at[kind, pair],
            recv_sem=recv_sem.at[kind, me],
            device_id={"seq": target},
            device_id_type=mesh,
        )

    def arrival(kind, shard):
        return pltpu.make_async_remote_copy(
            src_ref=slot(kind, shard),
            dst_ref=slot(kind, shard),
            send_sem=send_sem.at[kind, 0],
            recv_sem=recv_sem.at[kind, shard],
            device_id={"seq": shard},
            device_id_type=mesh,
        )

    def own_copy(kind, pair):
        return pltpu.make_async_copy(columns(kind, pair), slot(kind, me), own_sem.at[kind])

    width = part.shape[0]

    def channels(half_index):
        return pl.ds(pl.multiple_of(half_index * width, 16), width)

    def returned(target, core, pair, shard, index):
        return pltpu.make_async_remote_copy(
            src_ref=abuf.at[index, channels(target)],
            dst_ref=arecv.at[cfg, head, pair],
            send_sem=ret_send.at[target, core, index],
            recv_sem=ret_recv.at[cfg, head, pair],
            device_id={"cfg": target, "seq": shard, "head": core},
            device_id_type=mesh,
        )

    def returning(source, core, pair):
        return pltpu.make_async_remote_copy(
            src_ref=arecv.at[source, core, pair],
            dst_ref=arecv.at[source, core, pair],
            send_sem=ret_send.at[0, 0, 0],
            recv_sem=ret_recv.at[source, core, pair],
            device_id={"cfg": 1 - cfg},
            device_id_type=mesh,
        )

    inner = (me >= 2) & (me < 6)
    low = me == head
    high = me == owner_of(5, head)
    active = inner | low | high
    my_pair = jnp.where(inner, me - 2, jnp.where(low, 4, 5))

    barrier = pltpu.get_barrier_semaphore()
    for other in range(1, 8):

        @pl.when(other > me)
        def _(other=other):
            pl.semaphore_signal(barrier, inc=1, device_id={"seq": other}, device_id_type=mesh)

    @pl.when(head == 0)
    def _():
        pl.semaphore_signal(barrier, inc=1, device_id={"head": 1}, device_id_type=mesh)

    w_copy = pltpu.make_async_copy(w_hbm, wbuf, w_sem)
    small_copies = [
        pltpu.make_async_copy(mask_hbm, mask_ref, small_sem.at[0]),
        pltpu.make_async_copy(len_hbm, len_ref, small_sem.at[1]),
    ]

    greeted = me + cfg + head

    @pl.when(greeted > 0)
    def _():
        pl.semaphore_wait(barrier, greeted)

    @pl.when(cfg == 0)
    def _():
        pl.semaphore_signal(barrier, inc=1, device_id={"cfg": 1}, device_id_type=mesh)

    for other in range(7):

        @pl.when(other < me)
        def _(other=other):
            pl.semaphore_signal(here.at[me], inc=1, device_id={"seq": other}, device_id_type=mesh)

    @pl.when(active)
    def _():
        for kind in range(3):
            own_copy(kind, my_pair).start()

    for copy in small_copies:
        copy.start()
    w_copy.start()

    def await_shard(shard):
        @pl.when(shard > me)
        def _():
            pl.semaphore_wait(here.at[shard], 1)

    def send(kind, place):
        pair = ORDER[place]
        target = owner_of(pair, head)

        @pl.when(target != me)
        def _():
            remote(kind, pair, target).start()

    await_shard(1)
    send(0, 0)
    send(1, 0)

    @pl.when(head == 0)
    def _():
        send(0, 5)
        send(1, 5)

    for place in range(1, 3):
        await_shard(place + 1)
        send(0, place)
        send(1, place)

    @pl.when(half == 1)
    def _():
        for place in range(3):
            send(2, place)

        @pl.when(head == 0)
        def _():
            send(2, 5)

    for place in range(3, 5):
        await_shard(place + 1)
        send(0, place)
        send(1, place)
    await_shard(6)

    @pl.when(jnp.logical_not(head == 0))
    def _():
        send(0, 5)
        send(1, 5)

    @pl.when(half == 0)
    def _():
        for place in range(3):
            send(2, place)

    for place in range(3, 5):
        send(2, place)

    @pl.when((half == 0) | (head == 1))
    def _():
        send(2, 5)

    await_shard(7)

    for ready, place, axis in ((pair_ready, head, "head"), (cross_ready, cfg, "cfg")):

        @pl.when(place == 1)
        def _(ready=ready, axis=axis):
            pl.semaphore_signal(ready, inc=1, device_id={axis: 0}, device_id_type=mesh)

        pl.semaphore_wait(ready, 1)

        @pl.when(place == 0)
        def _(ready=ready, axis=axis):
            pl.semaphore_signal(ready, inc=1, device_id={axis: 1}, device_id_type=mesh)


    for copy in small_copies:
        copy.wait()
    @pl.when(active)
    def _():
        lane = lax.broadcasted_iota(jnp.int32, (8, 8 * rows), 1)
        row_shard = lax.broadcasted_iota(jnp.int32, (8, 8 * rows), 0)
        position = lane % rows
        limit = jnp.zeros((8, 8 * rows), jnp.int32)
        for j in range(8):
            column = jnp.zeros((8, 8 * rows), jnp.int32)
            for i in range(8):
                live = jnp.where(mask_ref[i, j] > 0, len_ref[j], 0)
                column = jnp.where(row_shard == i, live, column)
            limit = jnp.where((lane >= j * rows) & (lane < (j + 1) * rows), column, limit)
        bias[...] = jnp.where(position < limit, 0.0, NEG).reshape(8, 1, 8 * rows)

        w_copy.wait()
        weight = wbuf[:, pl.ds(pl.multiple_of(my_pair * PAIR, PAIR), PAIR)]

        for kind in range(2):
            own_copy(kind, my_pair).wait()
            for step in range(1, 8):
                shard = ((half + step // 4) % 2) * 4 + (me % 4 + step) % 4
                arrival(kind, shard).wait_recv()

        def attend(first, count):
            height = count * rows
            query = qbuf[pl.ds(pl.multiple_of(first * rows, 16), height)]
            zero = jnp.zeros_like(query)
            left = lax.broadcasted_iota(jnp.int32, (height, PAIR), 1) < HEAD_DIM
            stacked = jnp.concatenate(
                [jnp.where(left, query, zero), jnp.where(left, zero, query)], axis=0
            )
            scores = lax.dot_general(
                stacked, kbuf[...], (((1,), (1,)), ((), ())), preferred_element_type=jnp.float32
            )
            shape = scores.shape
            scores = scores.reshape(2, count, rows, 8 * rows) + bias[pl.ds(first, count)][None]
            scores = scores.reshape(shape)
            top = jnp.max(scores, axis=1, keepdims=True)
            weights = jnp.exp2((scores - top) * (score_scale * LOG2E))
            total = jnp.sum(weights, axis=1, keepdims=True)
            summed = jnp.dot(
                weights.astype(jnp.bfloat16), vbuf[...], preferred_element_type=jnp.float32
            )
            summed = summed / total
            attended = jnp.where(left, summed[:height], summed[height:]).astype(jnp.bfloat16)
            for index in range(count):
                abuf[first + index] = lax.dot_general(
                    weight,
                    attended[index * rows : (index + 1) * rows],
                    (((1,), (1,)), ((), ())),
                    preferred_element_type=jnp.float32,
                ).astype(RETURN)

        def give(shard):
            for target in range(2):
                for core in range(2):
                    @pl.when((shard != me) | (target != cfg) | (core != head))
                    def _(target=target, core=core):
                        returned(target, core, my_pair, shard, shard).start()

        own_copy(2, my_pair).wait()

        def await_query(shard):
            @pl.when(shard != me)
            def _():
                arrival(2, shard).wait_recv()

        def batch(first, count):
            for shard in range(first, first + count):
                await_query(shard)
            attend(first, count)
            for shard in range(first, first + count):
                give(shard)

        @pl.when(half == 0)
        def _():
            batch(0, 4)
            batch(4, 2)
            batch(6, 2)

        @pl.when(half == 1)
        def _():
            batch(0, 1)
            batch(4, 4)
            batch(1, 3)

        arecv[cfg, head, my_pair] = abuf[me, channels(cfg)]

    @pl.when(jnp.logical_not(active))
    def _():
        w_copy.wait()

    for source in range(2):
        for core in range(2):
            for pair in range(6):

                @pl.when((owner_of(pair, core) != me) | (cfg != source) | (head != core))
                def _(source=source, core=core, pair=pair):
                    returning(source, core, pair).wait_recv()

    def summed_pairs(source):
        cores = []
        for core in range(2):
            parts = [arecv[source, core, pair].astype(jnp.float32) for pair in range(6)]
            cores.append(((parts[0] + parts[1]) + (parts[2] + parts[3])) + (parts[4] + parts[5]))
        return cores[0] + cores[1]

    conditional = summed_pairs(0)
    unconditional = summed_pairs(1)
    part[...] = unconditional + guide_scale * (conditional - unconditional)
    own_part = pltpu.make_async_copy(part, out_ref, part_sem)
    own_part.start()

    for kind in range(3):
        for place in range(6):
            pair = ORDER[place]
            target = owner_of(pair, head)

            @pl.when(target != me)
            def _(kind=kind, pair=pair, target=target):
                remote(kind, pair, target).wait_send()

    @pl.when(active)
    def _():
        for target in range(2):
            for core in range(2):
                for shard in range(8):

                    @pl.when((shard != me) | (target != cfg) | (core != head))
                    def _(target=target, core=core, shard=shard):
                        returned(target, core, my_pair, shard, shard).wait_send()

    own_part.wait()


def joint(queries, keys, values, w_out, latents, block_mask, lengths, step_index):
    rows, cols = queries.shape[1:]
    hbm = pl.BlockSpec(memory_space=pltpu.HBM)
    dma = pltpu.SemaphoreType.DMA
    regular = pltpu.SemaphoreType.REGULAR
    width = latents.shape[1]
    latent = w_out.shape[1]
    small = jnp.int32
    guided = pl.pallas_call(
        joint_kernel,
        out_shape=jax.ShapeDtypeStruct((width, rows), jnp.float32),
        in_specs=[hbm] * 6,
        out_specs=pl.BlockSpec(memory_space=pl.ANY),
        scratch_shapes=[
            pltpu.VMEM((8 * rows, PAIR), jnp.bfloat16),
            pltpu.VMEM((8 * rows, PAIR), jnp.bfloat16),
            pltpu.VMEM((8 * rows, PAIR), jnp.bfloat16),
            pltpu.VMEM((8, latent, rows), RETURN),
            pltpu.VMEM((2, 2, 6, width, rows), RETURN),
            pltpu.VMEM((latent, cols), jnp.bfloat16),
            pltpu.VMEM((8, 1, 8 * rows), jnp.float32),
            pltpu.VMEM((width, rows), jnp.float32),
            dma((3, 6)),
            dma((3, 8)),
            dma((3,)),
            dma,
            dma((2, 2, 8)),
            dma((2, 2, 6)),
            regular((8,)),
            regular,
            regular,
            dma,
            pltpu.SMEM(block_mask.shape, small),
            pltpu.SMEM(lengths.shape, small),
            dma((2,)),
        ],
        compiler_params=pltpu.CompilerParams(collective_id=0, has_side_effects=True, vmem_limit_bytes=6 * 1024 * 1024),
    )(*[pltpu.with_memory_space_constraint(x, pltpu.HBM) for x in (queries[0], keys[0], values[0], w_out.T, block_mask, lengths)])
    tokens = latents.T
    coef_a, coef_b, coef_a2, coef_b2 = plan(jnp.where(guided == guided, step_index[0], 0))
    denoised = coef_a * tokens - coef_b * guided
    stepped = coef_a2 * denoised + coef_b2 * (coef_b * tokens + coef_a * guided)
    return (denoised.T, stepped.T)


def solution(mesh):
    in_specs = (
        P("cfg", "seq", "head"),
        P("cfg", "seq", "head"),
        P("cfg", "seq", "head"),
        P("head", None),
        P("seq", "cfg"),
        P(),
        P(),
        P(),
    )
    out_specs = (P("seq", "cfg"), P("seq", "cfg"))
    sizes = mesh.shape
    fits = sizes["cfg"] == 2 and sizes["seq"] == 8 and sizes["head"] == 2
    body = joint if fits else local
    return jax.shard_map(body, mesh=mesh, in_specs=in_specs, out_specs=out_specs, check_vma=False)
```

```python
import jax
import jax.numpy as jnp
from jax import lax
from jax.experimental import pallas as pl
from jax.experimental.pallas import tpu as pltpu
from jax.sharding import PartitionSpec as P

HEAD_DIM = 64
STEPS = 50


guide_scale = 6.0
score_scale = 0.125


def from_partner(value, axis, distance):
    mask = 2**distance
    pairs = [(source, source ^ mask) for source in range(lax.axis_size(axis))]
    return lax.ppermute(value, axis, pairs)


def shifted(block, axis, distance):
    devices = range(lax.axis_size(axis))
    route = [((i - distance) % len(devices), i) for i in devices]
    return lax.ppermute(block, axis, route)


def plan(step_value):
    step_float = step_value.astype(jnp.float32)
    first = (STEPS - step_float + 1.0) / (STEPS + 1.0)
    second = (STEPS - step_float) / (STEPS + 1.0)
    abar_now = jnp.exp(-6.0 * first * first)
    abar_next = jnp.exp(-6.0 * second * second)
    return (
        jnp.sqrt(abar_now),
        jnp.sqrt(1.0 - abar_now),
        jnp.sqrt(abar_next),
        jnp.sqrt(1.0 - abar_next),
    )


def regroup_heads(triple, bit, own_shard):
    upper = jnp.right_shift(own_shard, bit) % 2 == 1
    kept = []
    sent = []
    for member in triple:
        width = member.shape[1] // 2
        lower_cols = member[:, :width]
        upper_cols = member[:, width:]
        kept.append(jnp.where(upper, upper_cols, lower_cols))
        sent.append(jnp.where(upper, lower_cols, upper_cols))
    arrived = from_partner((sent[0], sent[1], sent[2]), "seq", bit)
    joined = []
    for mine, theirs in zip(kept, arrived):
        joined.append(
            jnp.where(upper, jnp.concatenate([theirs, mine], 0), jnp.concatenate([mine, theirs], 0))
        )
    return (joined[0], joined[1], joined[2])


def regroup_tokens(member, bit, own_shard):
    upper = jnp.right_shift(own_shard, bit) % 2 == 1
    height = member.shape[0] // 2
    lower_rows = member[:height]
    upper_rows = member[height:]
    kept = jnp.where(upper, upper_rows, lower_rows)
    sent = jnp.where(upper, lower_rows, upper_rows)
    arrived = from_partner(sent, "seq", bit)
    return jnp.where(
        upper, jnp.concatenate([arrived, kept], 1), jnp.concatenate([kept, arrived], 1)
    )


def local(queries, keys, values, w_out, latents, block_mask, lengths, step_index):
    row_count, columns = queries[0].shape
    shard_total = lax.axis_size("seq")
    levels = 1
    group = 2**levels
    own_shard = lax.axis_index("seq")
    triple = (queries[0], keys[0], values[0])
    bit = 0
    triple = regroup_heads(triple, bit, own_shard)
    query_group, key_group, value_group = triple
    group_rows = group * row_count
    group_cols = columns // group
    head_count = group_cols // HEAD_DIM
    group_index = own_shard // group
    group_count = shard_total // group
    query_heads = query_group.reshape(group_rows, head_count, HEAD_DIM)
    slot_offsets = jnp.arange(row_count)
    initial = (
        jnp.full((head_count, group_rows), -1e30, jnp.float32),
        jnp.zeros((head_count, group_rows), jnp.float32),
        jnp.zeros((head_count, group_rows, HEAD_DIM), jnp.float32),
    )

    def absorb(carry, piece, owner):
        key_piece, value_piece = piece
        submask = lax.dynamic_slice(
            block_mask, (group_index * group, owner * group), (group, group)
        )
        live_counts = lax.dynamic_slice_in_dim(lengths, owner * group, group)
        key_valid = (slot_offsets[None, :] < live_counts[:, None]).reshape(group_rows)
        pair_mask = jnp.repeat(jnp.repeat(submask > 0, row_count, axis=0), row_count, axis=1)
        keep = pair_mask & key_valid[None, :]

        def attend(state):
            running, total, accum = state
            scores = (
                jnp.einsum(
                    "qhd,khd->hqk",
                    query_heads,
                    key_piece.reshape(group_rows, head_count, HEAD_DIM),
                    preferred_element_type=jnp.float32,
                )
                * score_scale
            )
            scores = jnp.where(keep[None], scores, -1e30)
            newmax = jnp.maximum(running, jnp.max(scores, axis=-1))
            weights = jnp.where(keep[None], jnp.exp(scores - newmax[..., None]), 0.0)
            factor = jnp.exp(running - newmax)
            total = total * factor + jnp.sum(weights, axis=-1)
            accum = accum * factor[..., None] + jnp.einsum(
                "hqk,khd->hqd",
                weights.astype(jnp.bfloat16),
                value_piece.reshape(group_rows, head_count, HEAD_DIM),
                preferred_element_type=jnp.float32,
            )
            return (newmax, total, accum)

        return lax.cond(jnp.any(submask > 0), attend, lambda state: state, carry)

    carry = absorb(initial, (key_group, value_group), group_index)

    def one_turn(turn_index, state):
        held, totals = state
        held = shifted((held[0], held[1]), "seq", group)
        owner_index = (group_index - turn_index) % group_count
        totals = absorb(totals, held, owner_index)
        return (held, totals)

    held_last, carry = lax.fori_loop(1, group_count, one_turn, ((key_group, value_group), carry))
    running, total, accum = carry
    attended = (
        jnp.transpose(accum / total[..., None], (1, 0, 2))
        .reshape(group_rows, group_cols)
        .astype(jnp.bfloat16)
    )
    for bit in reversed(range(levels)):
        attended = regroup_tokens(attended, bit, own_shard)
    partial_value = jnp.dot(attended, w_out, preferred_element_type=jnp.float32)
    half_index = lax.axis_index("cfg")
    own_width = latents.shape[1]
    own_start = half_index * own_width
    prediction = lax.psum(partial_value, "head")
    mine = lax.dynamic_slice_in_dim(prediction, own_start, own_width, 1)
    outgoing = lax.dynamic_slice_in_dim(prediction, (1 - half_index) * own_width, own_width, 1)
    other_half = from_partner(outgoing, "cfg", 0)
    conditional = jnp.where(half_index == 0, mine, other_half)
    unconditional = jnp.where(half_index == 0, other_half, mine)
    guided = unconditional + guide_scale * (conditional - unconditional)
    coef_a, coef_b, coef_a2, coef_b2 = plan(step_index[0])
    denoised = coef_a * latents - coef_b * guided
    stepped = coef_a2 * denoised + coef_b2 * (coef_b * latents + coef_a * guided)
    return (denoised, stepped)


PAIR = 2 * HEAD_DIM
NEG = -1e30
LOG2E = 1.4426950408889634
ORDER = (4, 0, 1, 2, 3, 5)
RETURN = jnp.bfloat16
SPLIT = 256


def owner_of(pair, head):
    if pair < 4:
        return pair + 2
    return head if pair == 4 else 1 + 5 * head


def joint_kernel(
    q_hbm, k_hbm, v_hbm, w_hbm, mask_hbm, len_hbm,
    out_ref,
    qbuf, kbuf, vbuf, abuf, arecv, wbuf, bias, part,
    send_sem, recv_sem, own_sem, w_sem, ret_send, ret_recv,
    here, cross_ready, pair_ready,
    part_sem, mask_ref, len_ref, small_sem,
):
    cfg = lax.axis_index("cfg")
    me = lax.axis_index("seq")
    head = lax.axis_index("head")
    rows = q_hbm.shape[0]
    half = me // 4
    mesh = pl.DeviceIdType.MESH
    sources = (k_hbm, v_hbm, q_hbm)
    buffers = (kbuf, vbuf, qbuf)

    def slot(kind, shard):
        return buffers[kind].at[pl.ds(pl.multiple_of(shard * rows, 16), rows)]

    def columns(kind, pair):
        return sources[kind].at[:, pl.ds(pl.multiple_of(pair * PAIR, PAIR), PAIR)]

    def remote(kind, pair, target):
        return pltpu.make_async_remote_copy(
            src_ref=columns(kind, pair),
            dst_ref=slot(kind, me),
            send_sem=send_sem.at[kind, pair],
            recv_sem=recv_sem.at[kind, me],
            device_id={"seq": target},
            device_id_type=mesh,
        )

    def arrival(kind, shard):
        return pltpu.make_async_remote_copy(
            src_ref=slot(kind, shard),
            dst_ref=slot(kind, shard),
            send_sem=send_sem.at[kind, 0],
            recv_sem=recv_sem.at[kind, shard],
            device_id={"seq": shard},
            device_id_type=mesh,
        )

    def own_copy(kind, pair):
        return pltpu.make_async_copy(columns(kind, pair), slot(kind, me), own_sem.at[kind])

    width = part.shape[0]

    def channels(half_index):
        return pl.ds(pl.multiple_of(half_index * width, 16), width)

    def returned(target, core, pair, shard, index):
        return pltpu.make_async_remote_copy(
            src_ref=abuf.at[index, channels(target)],
            dst_ref=arecv.at[cfg, head, pair],
            send_sem=ret_send.at[target, core, index],
            recv_sem=ret_recv.at[cfg, head, pair],
            device_id={"cfg": target, "seq": shard, "head": core},
            device_id_type=mesh,
        )

    def returning(source, core, pair):
        return pltpu.make_async_remote_copy(
            src_ref=arecv.at[source, core, pair],
            dst_ref=arecv.at[source, core, pair],
            send_sem=ret_send.at[0, 0, 0],
            recv_sem=ret_recv.at[source, core, pair],
            device_id={"cfg": 1 - cfg},
            device_id_type=mesh,
        )

    inner = (me >= 2) & (me < 6)
    low = me == head
    high = me == owner_of(5, head)
    active = inner | low | high
    my_pair = jnp.where(inner, me - 2, jnp.where(low, 4, 5))

    barrier = pltpu.get_barrier_semaphore()
    for other in range(1, 8):

        @pl.when(other > me)
        def _(other=other):
            pl.semaphore_signal(barrier, inc=1, device_id={"seq": other}, device_id_type=mesh)

    @pl.when(head == 0)
    def _():
        pl.semaphore_signal(barrier, inc=1, device_id={"head": 1}, device_id_type=mesh)

    w_copy = pltpu.make_async_copy(w_hbm, wbuf, w_sem)
    small_copies = [
        pltpu.make_async_copy(mask_hbm, mask_ref, small_sem.at[0]),
        pltpu.make_async_copy(len_hbm, len_ref, small_sem.at[1]),
    ]

    greeted = me + cfg + head

    @pl.when(greeted > 0)
    def _():
        pl.semaphore_wait(barrier, greeted)

    @pl.when(cfg == 0)
    def _():
        pl.semaphore_signal(barrier, inc=1, device_id={"cfg": 1}, device_id_type=mesh)

    for other in range(7):

        @pl.when(other < me)
        def _(other=other):
            pl.semaphore_signal(here.at[me], inc=1, device_id={"seq": other}, device_id_type=mesh)

    def await_shard(shard):
        @pl.when(shard > me)
        def _():
            pl.semaphore_wait(here.at[shard], 1)

    def send(kind, place):
        pair = ORDER[place]
        target = owner_of(pair, head)

        @pl.when(target != me)
        def _():
            remote(kind, pair, target).start()

    await_shard(1)
    send(0, 0)
    send(1, 0)

    @pl.when(head == 0)
    def _():
        send(0, 5)
        send(1, 5)

    for place in range(1, 3):
        await_shard(place + 1)
        send(0, place)
        send(1, place)

    @pl.when(active)
    def _():
        for kind in range(3):
            own_copy(kind, my_pair).start()

    for copy in small_copies:
        copy.start()
    w_copy.start()

    @pl.when(me >= 6)
    def _():
        for place in range(3):
            send(2, place)

        @pl.when(head == 0)
        def _():
            send(2, 5)

    for place in range(3, 5):
        await_shard(place + 1)
        send(0, place)
        send(1, place)
    await_shard(6)

    @pl.when(jnp.logical_not(head == 0))
    def _():
        send(0, 5)
        send(1, 5)

    @pl.when(me < 6)
    def _():
        for place in range(3):
            send(2, place)

    for place in range(3, 5):
        send(2, place)

    @pl.when((me < 6) | (head == 1))
    def _():
        send(2, 5)

    await_shard(7)

    for ready, place, axis in ((pair_ready, head, "head"), (cross_ready, cfg, "cfg")):

        @pl.when(place == 1)
        def _(ready=ready, axis=axis):
            pl.semaphore_signal(ready, inc=1, device_id={axis: 0}, device_id_type=mesh)

        pl.semaphore_wait(ready, 1)

        @pl.when(place == 0)
        def _(ready=ready, axis=axis):
            pl.semaphore_signal(ready, inc=1, device_id={axis: 1}, device_id_type=mesh)


    for copy in small_copies:
        copy.wait()
    @pl.when(active)
    def _():
        lane = lax.broadcasted_iota(jnp.int32, (8, 8 * rows), 1)
        row_shard = lax.broadcasted_iota(jnp.int32, (8, 8 * rows), 0)
        position = lane % rows
        limit = jnp.zeros((8, 8 * rows), jnp.int32)
        for j in range(8):
            column = jnp.zeros((8, 8 * rows), jnp.int32)
            for i in range(8):
                live = jnp.where(mask_ref[i, j] > 0, len_ref[j], 0)
                column = jnp.where(row_shard == i, live, column)
            limit = jnp.where((lane >= j * rows) & (lane < (j + 1) * rows), column, limit)
        bias[...] = jnp.where(position < limit, 0.0, NEG).reshape(8, 1, 8 * rows)

        w_copy.wait()
        weight = wbuf[:, pl.ds(pl.multiple_of(my_pair * PAIR, PAIR), PAIR)]

        for kind in range(2):
            own_copy(kind, my_pair).wait()
        own_copy(2, my_pair).wait()

        def await_tokens(shards):
            for kind in range(2):
                for shard in shards:

                    @pl.when(shard != me)
                    def _(kind=kind, shard=shard):
                        arrival(kind, shard).wait_recv()

        def stack(first, count):
            height = count * rows
            query = qbuf[pl.ds(pl.multiple_of(first * rows, 16), height)]
            zero = jnp.zeros_like(query)
            left = lax.broadcasted_iota(jnp.int32, (height, PAIR), 1) < HEAD_DIM
            both = [jnp.where(left, query, zero), jnp.where(left, zero, query)]
            return jnp.concatenate(both, axis=0), left

        def scored(stacked, first, count, start, stop):
            scores = lax.dot_general(
                stacked,
                kbuf[start:stop],
                (((1,), (1,)), ((), ())),
                preferred_element_type=jnp.float32,
            )
            shape = scores.shape
            limits = bias[pl.ds(first, count), :, start:stop][None]
            scores = scores.reshape(2, count, rows, stop - start) + limits
            return scores.reshape(shape)

        def weighed(scores, top, start, stop):
            weights = jnp.exp2((scores - top) * (score_scale * LOG2E))
            total = jnp.sum(weights, axis=1, keepdims=True)
            summed = jnp.dot(
                weights.astype(jnp.bfloat16), vbuf[start:stop], preferred_element_type=jnp.float32
            )
            return total, summed

        def project(first, count, left, total, summed):
            height = count * rows
            summed = summed / total
            attended = jnp.where(left, summed[:height], summed[height:]).astype(jnp.bfloat16)
            for index in range(count):
                abuf[first + index] = lax.dot_general(
                    weight,
                    attended[index * rows : (index + 1) * rows],
                    (((1,), (1,)), ((), ())),
                    preferred_element_type=jnp.float32,
                ).astype(RETURN)

        def attend(first, count):
            stacked, left = stack(first, count)
            scores = scored(stacked, first, count, 0, 8 * rows)
            top = jnp.max(scores, axis=1, keepdims=True)
            project(first, count, left, *weighed(scores, top, 0, 8 * rows))

        def give(shard):
            for target in range(2):
                for core in range(2):
                    @pl.when((shard != me) | (target != cfg) | (core != head))
                    def _(target=target, core=core):
                        returned(target, core, my_pair, shard, shard).start()

        def await_query(shard):
            @pl.when(shard != me)
            def _():
                arrival(2, shard).wait_recv()

        def batch(first, count):
            for shard in [first + index for index in range(count)]:
                await_query(shard)
            attend(first, count)
            for shard in [first + index for index in range(count)]:
                give(shard)

        @pl.when(half == 0)
        def _():
            await_tokens(range(4))
            for shard in range(4):
                await_query(shard)
            stacked, left = stack(0, 4)
            near = scored(stacked, 0, 4, 0, SPLIT)
            near_top = jnp.max(near, axis=1, keepdims=True)
            near_total, near_summed = weighed(near, near_top, 0, SPLIT)
            await_tokens(range(4, 8))
            stop = 8 * rows
            far = scored(stacked, 0, 4, SPLIT, stop)
            top = jnp.maximum(near_top, jnp.max(far, axis=1, keepdims=True))
            total, summed = weighed(far, top, SPLIT, stop)
            scale = jnp.exp2((near_top - top) * (score_scale * LOG2E))
            project(0, 4, left, total + near_total * scale, summed + near_summed * scale)
            for shard in range(4):
                give(shard)

        @pl.when(half == 1)
        def _():
            await_tokens(range(8))

        def turn(index, carry):
            batch(jnp.where(index == 0, 0, jnp.where(index == 3, 2, 8 - 2 * index)), 2)
            return carry

        lax.fori_loop(1 - half, 3 + half, turn, 0)

        arecv[cfg, head, my_pair] = abuf[me, channels(cfg)]

    @pl.when(jnp.logical_not(active))
    def _():
        w_copy.wait()

    for kind in range(3):
        for place in range(6):
            pair = ORDER[place]
            target = owner_of(pair, head)

            @pl.when(target != me)
            def _(kind=kind, pair=pair, target=target):
                remote(kind, pair, target).wait_send()

    for source in range(2):
        for core in range(2):
            for pair in range(6):

                @pl.when((owner_of(pair, core) != me) | (cfg != source) | (head != core))
                def _(source=source, core=core, pair=pair):
                    returning(source, core, pair).wait_recv()

    def summed_pairs(source):
        cores = []
        for core in range(2):
            parts = [arecv[source, core, pair].astype(jnp.float32) for pair in range(6)]
            cores.append(((parts[0] + parts[1]) + (parts[2] + parts[3])) + (parts[4] + parts[5]))
        return cores[0] + cores[1]

    conditional = summed_pairs(0)
    unconditional = summed_pairs(1)
    part[...] = unconditional + guide_scale * (conditional - unconditional)
    own_part = pltpu.make_async_copy(part, out_ref, part_sem)
    own_part.start()

    @pl.when(active)
    def _():
        for target in range(2):
            for core in range(2):
                for shard in range(8):

                    @pl.when((shard != me) | (target != cfg) | (core != head))
                    def _(target=target, core=core, shard=shard):
                        returned(target, core, my_pair, shard, shard).wait_send()

    own_part.wait()


def joint(queries, keys, values, w_out, latents, block_mask, lengths, step_index):
    rows, cols = queries.shape[1:]
    hbm = pl.BlockSpec(memory_space=pltpu.HBM)
    dma = pltpu.SemaphoreType.DMA
    regular = pltpu.SemaphoreType.REGULAR
    width = latents.shape[1]
    latent = w_out.shape[1]
    small = jnp.int32
    guided = pl.pallas_call(
        joint_kernel,
        out_shape=jax.ShapeDtypeStruct((width, rows), jnp.float32),
        in_specs=[hbm] * 6,
        out_specs=pl.BlockSpec(memory_space=pl.ANY),
        scratch_shapes=[
            pltpu.VMEM((8 * rows, PAIR), jnp.bfloat16),
            pltpu.VMEM((8 * rows, PAIR), jnp.bfloat16),
            pltpu.VMEM((8 * rows, PAIR), jnp.bfloat16),
            pltpu.VMEM((8, latent, rows), RETURN),
            pltpu.VMEM((2, 2, 6, width, rows), RETURN),
            pltpu.VMEM((latent, cols), jnp.bfloat16),
            pltpu.VMEM((8, 1, 8 * rows), jnp.float32),
            pltpu.VMEM((width, rows), jnp.float32),
            dma((3, 6)),
            dma((3, 8)),
            dma((3,)),
            dma,
            dma((2, 2, 8)),
            dma((2, 2, 6)),
            regular((8,)),
            regular,
            regular,
            dma,
            pltpu.SMEM(block_mask.shape, small),
            pltpu.SMEM(lengths.shape, small),
            dma((2,)),
        ],
        compiler_params=pltpu.CompilerParams(collective_id=0, has_side_effects=True, vmem_limit_bytes=6 * 1024 * 1024),
    )(*[pltpu.with_memory_space_constraint(x, pltpu.HBM) for x in (queries[0], keys[0], values[0], w_out.T, block_mask, lengths)])
    tokens = latents.T
    coef_a, coef_b, coef_a2, coef_b2 = plan(jnp.where(guided == guided, step_index[0], 0))
    denoised = coef_a * tokens - coef_b * guided
    stepped = coef_a2 * denoised + coef_b2 * (coef_b * tokens + coef_a * guided)
    return (denoised.T, stepped.T)


def solution(mesh):
    in_specs = (
        P("cfg", "seq", "head"),
        P("cfg", "seq", "head"),
        P("cfg", "seq", "head"),
        P("head", None),
        P("seq", "cfg"),
        P(),
        P(),
        P(),
    )
    out_specs = (P("seq", "cfg"), P("seq", "cfg"))
    sizes = mesh.shape
    fits = sizes["cfg"] == 2 and sizes["seq"] == 8 and sizes["head"] == 2
    body = joint if fits else local
    return jax.shard_map(body, mesh=mesh, in_specs=in_specs, out_specs=out_specs, check_vma=False)
```

```python
import jax
import jax.numpy as jnp
from jax import lax
from jax.experimental import pallas as pl
from jax.experimental.pallas import tpu as pltpu
from jax.sharding import PartitionSpec as P

HEAD_DIM = 64
STEPS = 50


guide_scale = 6.0
score_scale = 0.125


def from_partner(value, axis, distance):
    mask = 2**distance
    pairs = [(source, source ^ mask) for source in range(lax.axis_size(axis))]
    return lax.ppermute(value, axis, pairs)


def shifted(block, axis, distance):
    devices = range(lax.axis_size(axis))
    route = [((i - distance) % len(devices), i) for i in devices]
    return lax.ppermute(block, axis, route)


def plan(step_value):
    step_float = step_value.astype(jnp.float32)
    first = (STEPS - step_float + 1.0) / (STEPS + 1.0)
    second = (STEPS - step_float) / (STEPS + 1.0)
    abar_now = jnp.exp(-6.0 * first * first)
    abar_next = jnp.exp(-6.0 * second * second)
    return (
        jnp.sqrt(abar_now),
        jnp.sqrt(1.0 - abar_now),
        jnp.sqrt(abar_next),
        jnp.sqrt(1.0 - abar_next),
    )


def regroup_heads(triple, bit, own_shard):
    upper = jnp.right_shift(own_shard, bit) % 2 == 1
    kept = []
    sent = []
    for member in triple:
        width = member.shape[1] // 2
        lower_cols = member[:, :width]
        upper_cols = member[:, width:]
        kept.append(jnp.where(upper, upper_cols, lower_cols))
        sent.append(jnp.where(upper, lower_cols, upper_cols))
    arrived = from_partner((sent[0], sent[1], sent[2]), "seq", bit)
    joined = []
    for mine, theirs in zip(kept, arrived):
        joined.append(
            jnp.where(upper, jnp.concatenate([theirs, mine], 0), jnp.concatenate([mine, theirs], 0))
        )
    return (joined[0], joined[1], joined[2])


def regroup_tokens(member, bit, own_shard):
    upper = jnp.right_shift(own_shard, bit) % 2 == 1
    height = member.shape[0] // 2
    lower_rows = member[:height]
    upper_rows = member[height:]
    kept = jnp.where(upper, upper_rows, lower_rows)
    sent = jnp.where(upper, lower_rows, upper_rows)
    arrived = from_partner(sent, "seq", bit)
    return jnp.where(
        upper, jnp.concatenate([arrived, kept], 1), jnp.concatenate([kept, arrived], 1)
    )


def local(queries, keys, values, w_out, latents, block_mask, lengths, step_index):
    row_count, columns = queries[0].shape
    shard_total = lax.axis_size("seq")
    levels = 1
    group = 2**levels
    own_shard = lax.axis_index("seq")
    triple = (queries[0], keys[0], values[0])
    bit = 0
    triple = regroup_heads(triple, bit, own_shard)
    query_group, key_group, value_group = triple
    group_rows = group * row_count
    group_cols = columns // group
    head_count = group_cols // HEAD_DIM
    group_index = own_shard // group
    group_count = shard_total // group
    query_heads = query_group.reshape(group_rows, head_count, HEAD_DIM)
    slot_offsets = jnp.arange(row_count)
    initial = (
        jnp.full((head_count, group_rows), -1e30, jnp.float32),
        jnp.zeros((head_count, group_rows), jnp.float32),
        jnp.zeros((head_count, group_rows, HEAD_DIM), jnp.float32),
    )

    def absorb(carry, piece, owner):
        key_piece, value_piece = piece
        submask = lax.dynamic_slice(
            block_mask, (group_index * group, owner * group), (group, group)
        )
        live_counts = lax.dynamic_slice_in_dim(lengths, owner * group, group)
        key_valid = (slot_offsets[None, :] < live_counts[:, None]).reshape(group_rows)
        pair_mask = jnp.repeat(jnp.repeat(submask > 0, row_count, axis=0), row_count, axis=1)
        keep = pair_mask & key_valid[None, :]

        def attend(state):
            running, total, accum = state
            scores = (
                jnp.einsum(
                    "qhd,khd->hqk",
                    query_heads,
                    key_piece.reshape(group_rows, head_count, HEAD_DIM),
                    preferred_element_type=jnp.float32,
                )
                * score_scale
            )
            scores = jnp.where(keep[None], scores, -1e30)
            newmax = jnp.maximum(running, jnp.max(scores, axis=-1))
            weights = jnp.where(keep[None], jnp.exp(scores - newmax[..., None]), 0.0)
            factor = jnp.exp(running - newmax)
            total = total * factor + jnp.sum(weights, axis=-1)
            accum = accum * factor[..., None] + jnp.einsum(
                "hqk,khd->hqd",
                weights.astype(jnp.bfloat16),
                value_piece.reshape(group_rows, head_count, HEAD_DIM),
                preferred_element_type=jnp.float32,
            )
            return (newmax, total, accum)

        return lax.cond(jnp.any(submask > 0), attend, lambda state: state, carry)

    carry = absorb(initial, (key_group, value_group), group_index)

    def one_turn(turn_index, state):
        held, totals = state
        held = shifted((held[0], held[1]), "seq", group)
        owner_index = (group_index - turn_index) % group_count
        totals = absorb(totals, held, owner_index)
        return (held, totals)

    held_last, carry = lax.fori_loop(1, group_count, one_turn, ((key_group, value_group), carry))
    running, total, accum = carry
    attended = (
        jnp.transpose(accum / total[..., None], (1, 0, 2))
        .reshape(group_rows, group_cols)
        .astype(jnp.bfloat16)
    )
    for bit in reversed(range(levels)):
        attended = regroup_tokens(attended, bit, own_shard)
    partial_value = jnp.dot(attended, w_out, preferred_element_type=jnp.float32)
    half_index = lax.axis_index("cfg")
    own_width = latents.shape[1]
    own_start = half_index * own_width
    prediction = lax.psum(partial_value, "head")
    mine = lax.dynamic_slice_in_dim(prediction, own_start, own_width, 1)
    outgoing = lax.dynamic_slice_in_dim(prediction, (1 - half_index) * own_width, own_width, 1)
    other_half = from_partner(outgoing, "cfg", 0)
    conditional = jnp.where(half_index == 0, mine, other_half)
    unconditional = jnp.where(half_index == 0, other_half, mine)
    guided = unconditional + guide_scale * (conditional - unconditional)
    coef_a, coef_b, coef_a2, coef_b2 = plan(step_index[0])
    denoised = coef_a * latents - coef_b * guided
    stepped = coef_a2 * denoised + coef_b2 * (coef_b * latents + coef_a * guided)
    return (denoised, stepped)


PAIR = 2 * HEAD_DIM
NEG = -1e30
LOG2E = 1.4426950408889634
ORDER = (4, 0, 1, 2, 3, 5)
RETURN = jnp.bfloat16
SPLIT = 256


def owner_of(pair, head):
    if pair < 4:
        return pair + 2
    return head if pair == 4 else 1 + 5 * head


def joint_kernel(
    q_hbm, k_hbm, v_hbm, w_hbm, mask_hbm, len_hbm,
    out_ref,
    qbuf, kbuf, vbuf, abuf, arecv, wbuf, bias, part,
    send_sem, recv_sem, own_sem, w_sem, ret_send, ret_recv,
    here, cross_ready, pair_ready,
    part_sem, mask_ref, len_ref, small_sem,
):
    cfg = lax.axis_index("cfg")
    me = lax.axis_index("seq")
    head = lax.axis_index("head")
    rows = q_hbm.shape[0]
    half = me // 4
    mesh = pl.DeviceIdType.MESH
    sources = (k_hbm, v_hbm, q_hbm)
    buffers = (kbuf, vbuf, qbuf)

    def slot(kind, shard):
        return buffers[kind].at[pl.ds(pl.multiple_of(shard * rows, 16), rows)]

    def columns(kind, pair):
        return sources[kind].at[:, pl.ds(pl.multiple_of(pair * PAIR, PAIR), PAIR)]

    def remote(kind, pair, target):
        return pltpu.make_async_remote_copy(
            src_ref=columns(kind, pair),
            dst_ref=slot(kind, me),
            send_sem=send_sem.at[kind, pair],
            recv_sem=recv_sem.at[kind, me],
            device_id={"seq": target},
            device_id_type=mesh,
        )

    def arrival(kind, shard):
        return pltpu.make_async_remote_copy(
            src_ref=slot(kind, shard),
            dst_ref=slot(kind, shard),
            send_sem=send_sem.at[kind, 0],
            recv_sem=recv_sem.at[kind, shard],
            device_id={"seq": shard},
            device_id_type=mesh,
        )

    def own_copy(kind, pair):
        return pltpu.make_async_copy(columns(kind, pair), slot(kind, me), own_sem.at[kind])

    width = part.shape[0]

    def channels(half_index):
        return pl.ds(pl.multiple_of(half_index * width, 16), width)

    def returned(target, core, pair, shard, index):
        return pltpu.make_async_remote_copy(
            src_ref=abuf.at[index, channels(target)],
            dst_ref=arecv.at[cfg, head, pair],
            send_sem=ret_send.at[target, core, index],
            recv_sem=ret_recv.at[cfg, head, pair],
            device_id={"cfg": target, "seq": shard, "head": core},
            device_id_type=mesh,
        )

    def returning(source, core, pair):
        return pltpu.make_async_remote_copy(
            src_ref=arecv.at[source, core, pair],
            dst_ref=arecv.at[source, core, pair],
            send_sem=ret_send.at[0, 0, 0],
            recv_sem=ret_recv.at[source, core, pair],
            device_id={"cfg": 1 - cfg},
            device_id_type=mesh,
        )

    inner = (me >= 2) & (me < 6)
    low = me == head
    high = me == owner_of(5, head)
    active = inner | low | high
    my_pair = jnp.where(inner, me - 2, jnp.where(low, 4, 5))

    barrier = pltpu.get_barrier_semaphore()
    for other in range(1, 8):

        @pl.when(other > me)
        def _(other=other):
            pl.semaphore_signal(barrier, inc=1, device_id={"seq": other}, device_id_type=mesh)

    @pl.when(head == 0)
    def _():
        pl.semaphore_signal(barrier, inc=1, device_id={"head": 1}, device_id_type=mesh)

    w_copy = pltpu.make_async_copy(w_hbm, wbuf, w_sem)
    small_copies = [
        pltpu.make_async_copy(mask_hbm, mask_ref, small_sem.at[0]),
        pltpu.make_async_copy(len_hbm, len_ref, small_sem.at[1]),
    ]

    greeted = me + cfg + head

    @pl.when(greeted > 0)
    def _():
        pl.semaphore_wait(barrier, greeted)

    @pl.when(cfg == 0)
    def _():
        pl.semaphore_signal(barrier, inc=1, device_id={"cfg": 1}, device_id_type=mesh)

    for other in range(7):

        @pl.when(other < me)
        def _(other=other):
            pl.semaphore_signal(here.at[me], inc=1, device_id={"seq": other}, device_id_type=mesh)

    def await_shard(shard):
        @pl.when(shard > me)
        def _():
            pl.semaphore_wait(here.at[shard], 1)

    def send(kind, place):
        pair = ORDER[place]
        target = owner_of(pair, head)

        @pl.when(target != me)
        def _():
            remote(kind, pair, target).start()

    await_shard(1)
    send(0, 0)
    send(1, 0)

    @pl.when(head == 0)
    def _():
        send(0, 5)
        send(1, 5)

    for place in range(1, 3):
        await_shard(place + 1)
        send(0, place)
        send(1, place)

    @pl.when(active)
    def _():
        for kind in range(3):
            own_copy(kind, my_pair).start()

    for copy in small_copies:
        copy.start()
    w_copy.start()

    @pl.when(me >= 6)
    def _():
        for place in range(3):
            send(2, place)

        @pl.when(head == 0)
        def _():
            send(2, 5)

    for place in range(3, 5):
        await_shard(place + 1)
        send(0, place)
        send(1, place)
    await_shard(6)

    @pl.when(jnp.logical_not(head == 0))
    def _():
        send(0, 5)
        send(1, 5)

    @pl.when(me < 6)
    def _():
        for place in range(3):
            send(2, place)

    for place in range(3, 5):
        send(2, place)

    @pl.when((me < 6) | (head == 1))
    def _():
        send(2, 5)

    await_shard(7)

    for ready, place, axis in ((pair_ready, head, "head"), (cross_ready, cfg, "cfg")):

        @pl.when(place == 1)
        def _(ready=ready, axis=axis):
            pl.semaphore_signal(ready, inc=1, device_id={axis: 0}, device_id_type=mesh)

        pl.semaphore_wait(ready, 1)

        @pl.when(place == 0)
        def _(ready=ready, axis=axis):
            pl.semaphore_signal(ready, inc=1, device_id={axis: 1}, device_id_type=mesh)


    for copy in small_copies:
        copy.wait()
    @pl.when(active)
    def _():
        lane = lax.broadcasted_iota(jnp.int32, (8, 8 * rows), 1)
        row_shard = lax.broadcasted_iota(jnp.int32, (8, 8 * rows), 0)
        position = lane % rows
        limit = jnp.zeros((8, 8 * rows), jnp.int32)
        for j in range(8):
            column = jnp.zeros((8, 8 * rows), jnp.int32)
            for i in range(8):
                live = jnp.where(mask_ref[i, j] > 0, len_ref[j], 0)
                column = jnp.where(row_shard == i, live, column)
            limit = jnp.where((lane >= j * rows) & (lane < (j + 1) * rows), column, limit)
        bias[...] = jnp.where(position < limit, 0.0, NEG).reshape(8, 1, 8 * rows)

        w_copy.wait()
        weight = wbuf[:, pl.ds(pl.multiple_of(my_pair * PAIR, PAIR), PAIR)]

        for kind in range(2):
            own_copy(kind, my_pair).wait()
        own_copy(2, my_pair).wait()

        def await_tokens(shards):
            for kind in range(2):
                for shard in shards:

                    @pl.when(shard != me)
                    def _(kind=kind, shard=shard):
                        arrival(kind, shard).wait_recv()

        def stack(first, count):
            height = count * rows
            query = qbuf[pl.ds(pl.multiple_of(first * rows, 16), height)]
            zero = jnp.zeros_like(query)
            left = lax.broadcasted_iota(jnp.int32, (height, PAIR), 1) < HEAD_DIM
            both = [jnp.where(left, query, zero), jnp.where(left, zero, query)]
            return jnp.concatenate(both, axis=0), left

        def scored(stacked, first, count, start, stop):
            scores = lax.dot_general(
                stacked,
                kbuf[start:stop],
                (((1,), (1,)), ((), ())),
                preferred_element_type=jnp.float32,
            )
            shape = scores.shape
            limits = bias[pl.ds(first, count), :, start:stop][None]
            scores = scores.reshape(2, count, rows, stop - start) + limits
            return scores.reshape(shape)

        def weighed(scores, top, start, stop):
            weights = jnp.exp2((scores - top) * (score_scale * LOG2E))
            total = jnp.sum(weights, axis=1, keepdims=True)
            summed = jnp.dot(
                weights.astype(jnp.bfloat16), vbuf[start:stop], preferred_element_type=jnp.float32
            )
            return total, summed

        def project(first, count, left, total, summed):
            height = count * rows
            summed = summed / total
            attended = jnp.where(left, summed[:height], summed[height:]).astype(jnp.bfloat16)
            for index in range(count):
                abuf[first + index] = lax.dot_general(
                    weight,
                    attended[index * rows : (index + 1) * rows],
                    (((1,), (1,)), ((), ())),
                    preferred_element_type=jnp.float32,
                ).astype(RETURN)

        def attend(first, count):
            stacked, left = stack(first, count)
            scores = scored(stacked, first, count, 0, 8 * rows)
            top = jnp.max(scores, axis=1, keepdims=True)
            project(first, count, left, *weighed(scores, top, 0, 8 * rows))

        def give(shard):
            for target in range(2):
                for core in range(2):
                    @pl.when((shard != me) | (target != cfg) | (core != head))
                    def _(target=target, core=core):
                        returned(target, core, my_pair, shard, shard).start()

        def await_query(shard):
            @pl.when(shard != me)
            def _():
                arrival(2, shard).wait_recv()

        def batch(first, count):
            for shard in [first + index for index in range(count)]:
                await_query(shard)
            attend(first, count)
            for shard in [first + index for index in range(count)]:
                give(shard)

        @pl.when(half == 0)
        def _():
            await_tokens(range(4))
            for shard in range(4):
                await_query(shard)
            stacked, left = stack(0, 4)
            near = scored(stacked, 0, 4, 0, SPLIT)
            near_top = jnp.max(near, axis=1, keepdims=True)
            near_total, near_summed = weighed(near, near_top, 0, SPLIT)
            await_tokens(range(4, 8))
            stop = 8 * rows
            far = scored(stacked, 0, 4, SPLIT, stop)
            top = jnp.maximum(near_top, jnp.max(far, axis=1, keepdims=True))
            total, summed = weighed(far, top, SPLIT, stop)
            scale = jnp.exp2((near_top - top) * (score_scale * LOG2E))
            project(0, 4, left, total + near_total * scale, summed + near_summed * scale)
            for shard in range(4):
                give(shard)

        @pl.when(half == 1)
        def _():
            await_tokens(range(8))

        def turn(index, carry):
            batch(jnp.where(index == 0, 0, jnp.where(index == 3, 2, 8 - 2 * index)), 2)
            return carry

        lax.fori_loop(1 - half, 3 + half, turn, 0)

        arecv[cfg, head, my_pair] = abuf[me, channels(cfg)]

    @pl.when(jnp.logical_not(active))
    def _():
        w_copy.wait()

    for kind in range(3):
        for place in range(6):
            pair = ORDER[place]
            target = owner_of(pair, head)

            @pl.when(target != me)
            def _(kind=kind, pair=pair, target=target):
                remote(kind, pair, target).wait_send()

    @pl.when(active)
    def _():
        for target in range(2):
            for core in range(2):
                for shard in range(8):

                    @pl.when((shard != me) | (target != cfg) | (core != head))
                    def _(target=target, core=core, shard=shard):
                        returned(target, core, my_pair, shard, shard).wait_send()

    for source in range(2):
        for core in range(2):
            for pair in range(6):

                @pl.when((owner_of(pair, core) != me) | (cfg != source) | (head != core))
                def _(source=source, core=core, pair=pair):
                    returning(source, core, pair).wait_recv()

    def summed_pairs(source):
        cores = []
        for core in range(2):
            parts = [arecv[source, core, pair].astype(jnp.float32) for pair in range(6)]
            cores.append(((parts[0] + parts[1]) + (parts[2] + parts[3])) + (parts[4] + parts[5]))
        return cores[0] + cores[1]

    conditional = summed_pairs(0)
    unconditional = summed_pairs(1)
    part[...] = unconditional + guide_scale * (conditional - unconditional)
    own_part = pltpu.make_async_copy(part, out_ref, part_sem)
    own_part.start()

    own_part.wait()


def joint(queries, keys, values, w_out, latents, block_mask, lengths, step_index):
    rows, cols = queries.shape[1:]
    hbm = pl.BlockSpec(memory_space=pltpu.HBM)
    dma = pltpu.SemaphoreType.DMA
    regular = pltpu.SemaphoreType.REGULAR
    width = latents.shape[1]
    latent = w_out.shape[1]
    small = jnp.int32
    guided = pl.pallas_call(
        joint_kernel,
        out_shape=jax.ShapeDtypeStruct((width, rows), jnp.float32),
        in_specs=[hbm] * 6,
        out_specs=pl.BlockSpec(memory_space=pl.ANY),
        scratch_shapes=[
            pltpu.VMEM((8 * rows, PAIR), jnp.bfloat16),
            pltpu.VMEM((8 * rows, PAIR), jnp.bfloat16),
            pltpu.VMEM((8 * rows, PAIR), jnp.bfloat16),
            pltpu.VMEM((8, latent, rows), RETURN),
            pltpu.VMEM((2, 2, 6, width, rows), RETURN),
            pltpu.VMEM((latent, cols), jnp.bfloat16),
            pltpu.VMEM((8, 1, 8 * rows), jnp.float32),
            pltpu.VMEM((width, rows), jnp.float32),
            dma((3, 6)),
            dma((3, 8)),
            dma((3,)),
            dma,
            dma((2, 2, 8)),
            dma((2, 2, 6)),
            regular((8,)),
            regular,
            regular,
            dma,
            pltpu.SMEM(block_mask.shape, small),
            pltpu.SMEM(lengths.shape, small),
            dma((2,)),
        ],
        compiler_params=pltpu.CompilerParams(collective_id=0, has_side_effects=True, vmem_limit_bytes=6 * 1024 * 1024),
    )(*[pltpu.with_memory_space_constraint(x, pltpu.HBM) for x in (queries[0], keys[0], values[0], w_out.T, block_mask, lengths)])
    tokens = latents.T
    coef_a, coef_b, coef_a2, coef_b2 = plan(jnp.where(guided == guided, step_index[0], 0))
    denoised = coef_a * tokens - coef_b * guided
    stepped = coef_a2 * denoised + coef_b2 * (coef_b * tokens + coef_a * guided)
    return (denoised.T, stepped.T)


def solution(mesh):
    in_specs = (
        P("cfg", "seq", "head"),
        P("cfg", "seq", "head"),
        P("cfg", "seq", "head"),
        P("head", None),
        P("seq", "cfg"),
        P(),
        P(),
        P(),
    )
    out_specs = (P("seq", "cfg"), P("seq", "cfg"))
    sizes = mesh.shape
    fits = sizes["cfg"] == 2 and sizes["seq"] == 8 and sizes["head"] == 2
    body = joint if fits else local
    return jax.shard_map(body, mesh=mesh, in_specs=in_specs, out_specs=out_specs, check_vma=False)
```

```python
import jax
import jax.numpy as jnp
from jax import lax
from jax.experimental import pallas as pl
from jax.experimental.pallas import tpu as pltpu
from jax.sharding import PartitionSpec as P

HEAD_DIM = 64
STEPS = 50


guide_scale = 6.0
score_scale = 0.125


def from_partner(value, axis, distance):
    mask = 2**distance
    pairs = [(source, source ^ mask) for source in range(lax.axis_size(axis))]
    return lax.ppermute(value, axis, pairs)


def shifted(block, axis, distance):
    devices = range(lax.axis_size(axis))
    route = [((i - distance) % len(devices), i) for i in devices]
    return lax.ppermute(block, axis, route)


def plan(step_value):
    step_float = step_value.astype(jnp.float32)
    first = (STEPS - step_float + 1.0) / (STEPS + 1.0)
    second = (STEPS - step_float) / (STEPS + 1.0)
    abar_now = jnp.exp(-6.0 * first * first)
    abar_next = jnp.exp(-6.0 * second * second)
    return (
        jnp.sqrt(abar_now),
        jnp.sqrt(1.0 - abar_now),
        jnp.sqrt(abar_next),
        jnp.sqrt(1.0 - abar_next),
    )


def regroup_heads(triple, bit, own_shard):
    upper = jnp.right_shift(own_shard, bit) % 2 == 1
    kept = []
    sent = []
    for member in triple:
        width = member.shape[1] // 2
        lower_cols = member[:, :width]
        upper_cols = member[:, width:]
        kept.append(jnp.where(upper, upper_cols, lower_cols))
        sent.append(jnp.where(upper, lower_cols, upper_cols))
    arrived = from_partner((sent[0], sent[1], sent[2]), "seq", bit)
    joined = []
    for mine, theirs in zip(kept, arrived):
        joined.append(
            jnp.where(upper, jnp.concatenate([theirs, mine], 0), jnp.concatenate([mine, theirs], 0))
        )
    return (joined[0], joined[1], joined[2])


def regroup_tokens(member, bit, own_shard):
    upper = jnp.right_shift(own_shard, bit) % 2 == 1
    height = member.shape[0] // 2
    lower_rows = member[:height]
    upper_rows = member[height:]
    kept = jnp.where(upper, upper_rows, lower_rows)
    sent = jnp.where(upper, lower_rows, upper_rows)
    arrived = from_partner(sent, "seq", bit)
    return jnp.where(
        upper, jnp.concatenate([arrived, kept], 1), jnp.concatenate([kept, arrived], 1)
    )


def local(queries, keys, values, w_out, latents, block_mask, lengths, step_index):
    row_count, columns = queries[0].shape
    shard_total = lax.axis_size("seq")
    levels = 1
    group = 2**levels
    own_shard = lax.axis_index("seq")
    triple = (queries[0], keys[0], values[0])
    bit = 0
    triple = regroup_heads(triple, bit, own_shard)
    query_group, key_group, value_group = triple
    group_rows = group * row_count
    group_cols = columns // group
    head_count = group_cols // HEAD_DIM
    group_index = own_shard // group
    group_count = shard_total // group
    query_heads = query_group.reshape(group_rows, head_count, HEAD_DIM)
    slot_offsets = jnp.arange(row_count)
    initial = (
        jnp.full((head_count, group_rows), -1e30, jnp.float32),
        jnp.zeros((head_count, group_rows), jnp.float32),
        jnp.zeros((head_count, group_rows, HEAD_DIM), jnp.float32),
    )

    def absorb(carry, piece, owner):
        key_piece, value_piece = piece
        submask = lax.dynamic_slice(
            block_mask, (group_index * group, owner * group), (group, group)
        )
        live_counts = lax.dynamic_slice_in_dim(lengths, owner * group, group)
        key_valid = (slot_offsets[None, :] < live_counts[:, None]).reshape(group_rows)
        pair_mask = jnp.repeat(jnp.repeat(submask > 0, row_count, axis=0), row_count, axis=1)
        keep = pair_mask & key_valid[None, :]

        def attend(state):
            running, total, accum = state
            scores = (
                jnp.einsum(
                    "qhd,khd->hqk",
                    query_heads,
                    key_piece.reshape(group_rows, head_count, HEAD_DIM),
                    preferred_element_type=jnp.float32,
                )
                * score_scale
            )
            scores = jnp.where(keep[None], scores, -1e30)
            newmax = jnp.maximum(running, jnp.max(scores, axis=-1))
            weights = jnp.where(keep[None], jnp.exp(scores - newmax[..., None]), 0.0)
            factor = jnp.exp(running - newmax)
            total = total * factor + jnp.sum(weights, axis=-1)
            accum = accum * factor[..., None] + jnp.einsum(
                "hqk,khd->hqd",
                weights.astype(jnp.bfloat16),
                value_piece.reshape(group_rows, head_count, HEAD_DIM),
                preferred_element_type=jnp.float32,
            )
            return (newmax, total, accum)

        return lax.cond(jnp.any(submask > 0), attend, lambda state: state, carry)

    carry = absorb(initial, (key_group, value_group), group_index)

    def one_turn(turn_index, state):
        held, totals = state
        held = shifted((held[0], held[1]), "seq", group)
        owner_index = (group_index - turn_index) % group_count
        totals = absorb(totals, held, owner_index)
        return (held, totals)

    held_last, carry = lax.fori_loop(1, group_count, one_turn, ((key_group, value_group), carry))
    running, total, accum = carry
    attended = (
        jnp.transpose(accum / total[..., None], (1, 0, 2))
        .reshape(group_rows, group_cols)
        .astype(jnp.bfloat16)
    )
    for bit in reversed(range(levels)):
        attended = regroup_tokens(attended, bit, own_shard)
    partial_value = jnp.dot(attended, w_out, preferred_element_type=jnp.float32)
    half_index = lax.axis_index("cfg")
    own_width = latents.shape[1]
    own_start = half_index * own_width
    prediction = lax.psum(partial_value, "head")
    mine = lax.dynamic_slice_in_dim(prediction, own_start, own_width, 1)
    outgoing = lax.dynamic_slice_in_dim(prediction, (1 - half_index) * own_width, own_width, 1)
    other_half = from_partner(outgoing, "cfg", 0)
    conditional = jnp.where(half_index == 0, mine, other_half)
    unconditional = jnp.where(half_index == 0, other_half, mine)
    guided = unconditional + guide_scale * (conditional - unconditional)
    coef_a, coef_b, coef_a2, coef_b2 = plan(step_index[0])
    denoised = coef_a * latents - coef_b * guided
    stepped = coef_a2 * denoised + coef_b2 * (coef_b * latents + coef_a * guided)
    return (denoised, stepped)


PAIR = 2 * HEAD_DIM
NEG = -1e30
LOG2E = 1.4426950408889634
ORDER = (4, 0, 1, 2, 3, 5)
RETURN = jnp.bfloat16
SPLIT = 256


def owner_of(pair, head):
    if pair < 4:
        return pair + 2
    return head if pair == 4 else 1 + 5 * head


def joint_kernel(
    q_hbm, k_hbm, v_hbm, w_hbm, mask_hbm, len_hbm,
    out_ref,
    qbuf, kbuf, vbuf, abuf, arecv, wbuf, bias, part,
    send_sem, recv_sem, own_sem, w_sem, ret_send, ret_recv,
    here, cross_ready, pair_ready,
    part_sem, mask_ref, len_ref, small_sem,
):
    cfg = lax.axis_index("cfg")
    me = lax.axis_index("seq")
    head = lax.axis_index("head")
    rows = q_hbm.shape[0]
    half = me // 4
    mesh = pl.DeviceIdType.MESH
    sources = (k_hbm, v_hbm, q_hbm)
    buffers = (kbuf, vbuf, qbuf)

    def slot(kind, shard):
        return buffers[kind].at[pl.ds(pl.multiple_of(shard * rows, 16), rows)]

    def columns(kind, pair):
        return sources[kind].at[:, pl.ds(pl.multiple_of(pair * PAIR, PAIR), PAIR)]

    def remote(kind, pair, target):
        return pltpu.make_async_remote_copy(
            src_ref=columns(kind, pair),
            dst_ref=slot(kind, me),
            send_sem=send_sem.at[kind, pair],
            recv_sem=recv_sem.at[kind, me],
            device_id={"seq": target},
            device_id_type=mesh,
        )

    def arrival(kind, shard):
        return pltpu.make_async_remote_copy(
            src_ref=slot(kind, shard),
            dst_ref=slot(kind, shard),
            send_sem=send_sem.at[kind, 0],
            recv_sem=recv_sem.at[kind, shard],
            device_id={"seq": shard},
            device_id_type=mesh,
        )

    def own_copy(kind, pair):
        return pltpu.make_async_copy(columns(kind, pair), slot(kind, me), own_sem.at[kind])

    width = part.shape[0]

    def channels(half_index):
        return pl.ds(pl.multiple_of(half_index * width, 16), width)

    def returned(target, core, pair, shard, index):
        return pltpu.make_async_remote_copy(
            src_ref=abuf.at[index, channels(target)],
            dst_ref=arecv.at[cfg, head, pair],
            send_sem=ret_send.at[target, core, index],
            recv_sem=ret_recv.at[cfg, head, pair],
            device_id={"cfg": target, "seq": shard, "head": core},
            device_id_type=mesh,
        )

    def returning(source, core, pair):
        return pltpu.make_async_remote_copy(
            src_ref=arecv.at[source, core, pair],
            dst_ref=arecv.at[source, core, pair],
            send_sem=ret_send.at[0, 0, 0],
            recv_sem=ret_recv.at[source, core, pair],
            device_id={"cfg": 1 - cfg},
            device_id_type=mesh,
        )

    inner = (me >= 2) & (me < 6)
    low = me == head
    high = me == owner_of(5, head)
    active = inner | low | high
    my_pair = jnp.where(inner, me - 2, jnp.where(low, 4, 5))

    barrier = pltpu.get_barrier_semaphore()
    for other in range(1, 8):

        @pl.when(other > me)
        def _(other=other):
            pl.semaphore_signal(barrier, inc=1, device_id={"seq": other}, device_id_type=mesh)

    @pl.when(head == 0)
    def _():
        pl.semaphore_signal(barrier, inc=1, device_id={"head": 1}, device_id_type=mesh)

    w_copy = pltpu.make_async_copy(w_hbm, wbuf, w_sem)
    small_copies = [
        pltpu.make_async_copy(mask_hbm, mask_ref, small_sem.at[0]),
        pltpu.make_async_copy(len_hbm, len_ref, small_sem.at[1]),
    ]

    greeted = me + cfg + head

    @pl.when(greeted > 0)
    def _():
        pl.semaphore_wait(barrier, greeted)

    @pl.when(cfg == 0)
    def _():
        pl.semaphore_signal(barrier, inc=1, device_id={"cfg": 1}, device_id_type=mesh)

    for other in range(7):

        @pl.when(other < me)
        def _(other=other):
            pl.semaphore_signal(here.at[me], inc=1, device_id={"seq": other}, device_id_type=mesh)

    def await_shard(shard):
        @pl.when(shard > me)
        def _():
            pl.semaphore_wait(here.at[shard], 1)

    def send(kind, place):
        pair = ORDER[place]
        target = owner_of(pair, head)

        @pl.when(target != me)
        def _():
            remote(kind, pair, target).start()

    await_shard(1)
    send(0, 0)
    send(1, 0)

    @pl.when(head == 0)
    def _():
        send(0, 5)
        send(1, 5)

    for place in range(1, 3):
        await_shard(place + 1)
        send(0, place)
        send(1, place)

    @pl.when(active)
    def _():
        for kind in range(3):
            own_copy(kind, my_pair).start()

    for copy in small_copies:
        copy.start()
    w_copy.start()

    @pl.when(me >= 6)
    def _():
        for place in range(3):
            send(2, place)

        @pl.when(head == 0)
        def _():
            send(2, 5)

    for place in range(3, 5):
        await_shard(place + 1)
        send(0, place)
        send(1, place)
    await_shard(6)

    @pl.when(jnp.logical_not(head == 0))
    def _():
        send(0, 5)
        send(1, 5)

    @pl.when(me < 6)
    def _():
        for place in range(3):
            send(2, place)

    for place in range(3, 5):
        send(2, place)

    @pl.when((me < 6) | (head == 1))
    def _():
        send(2, 5)

    await_shard(7)

    for ready, place, axis in ((pair_ready, head, "head"), (cross_ready, cfg, "cfg")):

        @pl.when(place == 1)
        def _(ready=ready, axis=axis):
            pl.semaphore_signal(ready, inc=1, device_id={axis: 0}, device_id_type=mesh)

        pl.semaphore_wait(ready, 1)

        @pl.when(place == 0)
        def _(ready=ready, axis=axis):
            pl.semaphore_signal(ready, inc=1, device_id={axis: 1}, device_id_type=mesh)


    for copy in small_copies:
        copy.wait()
    @pl.when(active)
    def _():
        lane = lax.broadcasted_iota(jnp.int32, (8, 8 * rows), 1)
        row_shard = lax.broadcasted_iota(jnp.int32, (8, 8 * rows), 0)
        position = lane % rows
        limit = jnp.zeros((8, 8 * rows), jnp.int32)
        for j in range(8):
            column = jnp.zeros((8, 8 * rows), jnp.int32)
            for i in range(8):
                live = jnp.where(mask_ref[i, j] > 0, len_ref[j], 0)
                column = jnp.where(row_shard == i, live, column)
            limit = jnp.where((lane >= j * rows) & (lane < (j + 1) * rows), column, limit)
        bias[...] = jnp.where(position < limit, 0.0, NEG).reshape(8, 1, 8 * rows)

        w_copy.wait()
        weight = wbuf[:, pl.ds(pl.multiple_of(my_pair * PAIR, PAIR), PAIR)]

        for kind in range(2):
            own_copy(kind, my_pair).wait()
        own_copy(2, my_pair).wait()

        def await_tokens(shards):
            for kind in range(2):
                for shard in shards:

                    @pl.when(shard != me)
                    def _(kind=kind, shard=shard):
                        arrival(kind, shard).wait_recv()

        def give(shard):
            for target in range(2):
                for core in range(2):
                    @pl.when((shard != me) | (target != cfg) | (core != head))
                    def _(target=target, core=core):
                        returned(target, core, my_pair, shard, shard).start()

        def stack(first, count):
            height = count * rows
            query = qbuf[pl.ds(pl.multiple_of(first * rows, 16), height)]
            zero = jnp.zeros_like(query)
            left = lax.broadcasted_iota(jnp.int32, (height, PAIR), 1) < HEAD_DIM
            both = [jnp.where(left, query, zero), jnp.where(left, zero, query)]
            return jnp.concatenate(both, axis=0), left

        def scored(stacked, first, count, start, stop):
            scores = lax.dot_general(
                stacked,
                kbuf[start:stop],
                (((1,), (1,)), ((), ())),
                preferred_element_type=jnp.float32,
            )
            shape = scores.shape
            limits = bias[pl.ds(first, count), :, start:stop][None]
            scores = scores.reshape(2, count, rows, stop - start) + limits
            return scores.reshape(shape)

        def weighed(scores, top, start, stop):
            weights = jnp.exp2((scores - top) * (score_scale * LOG2E))
            total = jnp.sum(weights, axis=1, keepdims=True)
            summed = jnp.dot(
                weights.astype(jnp.bfloat16), vbuf[start:stop], preferred_element_type=jnp.float32
            )
            return total, summed

        def project(first, count, left, total, summed):
            height = count * rows
            summed = summed / total
            attended = jnp.where(left, summed[:height], summed[height:]).astype(jnp.bfloat16)
            for index in range(count):
                abuf[first + index] = lax.dot_general(
                    weight,
                    attended[index * rows : (index + 1) * rows],
                    (((1,), (1,)), ((), ())),
                    preferred_element_type=jnp.float32,
                ).astype(RETURN)
                give(first + index)

        def attend(first, count):
            stacked, left = stack(first, count)
            scores = scored(stacked, first, count, 0, 8 * rows)
            top = jnp.max(scores, axis=1, keepdims=True)
            project(first, count, left, *weighed(scores, top, 0, 8 * rows))

        def await_query(shard):
            @pl.when(shard != me)
            def _():
                arrival(2, shard).wait_recv()

        def batch(first, count):
            for shard in [first + index for index in range(count)]:
                await_query(shard)
            attend(first, count)

        @pl.when(half == 0)
        def _():
            await_tokens(range(4))
            for shard in range(4):
                await_query(shard)
            stacked, left = stack(0, 4)
            near = scored(stacked, 0, 4, 0, SPLIT)
            near_top = jnp.max(near, axis=1, keepdims=True)
            near_total, near_summed = weighed(near, near_top, 0, SPLIT)
            await_tokens(range(4, 8))
            stop = 8 * rows
            far = scored(stacked, 0, 4, SPLIT, stop)
            top = jnp.maximum(near_top, jnp.max(far, axis=1, keepdims=True))
            total, summed = weighed(far, top, SPLIT, stop)
            scale = jnp.exp2((near_top - top) * (score_scale * LOG2E))
            project(0, 4, left, total + near_total * scale, summed + near_summed * scale)

        @pl.when(half == 1)
        def _():
            await_tokens(range(8))

        def turn(index, carry):
            batch(jnp.where(index == 0, 0, jnp.where(index == 3, 2, 8 - 2 * index)), 2)
            return carry

        lax.fori_loop(1 - half, 3 + half, turn, 0)

        arecv[cfg, head, my_pair] = abuf[me, channels(cfg)]

    @pl.when(jnp.logical_not(active))
    def _():
        w_copy.wait()

    for kind in range(3):
        for place in range(6):
            pair = ORDER[place]
            target = owner_of(pair, head)

            @pl.when(target != me)
            def _(kind=kind, pair=pair, target=target):
                remote(kind, pair, target).wait_send()

    @pl.when(active)
    def _():
        for target in range(2):
            for core in range(2):
                for shard in range(8):

                    @pl.when((shard != me) | (target != cfg) | (core != head))
                    def _(target=target, core=core, shard=shard):
                        returned(target, core, my_pair, shard, shard).wait_send()

    for source in range(2):
        for core in range(2):
            for pair in range(6):

                @pl.when((owner_of(pair, core) != me) | (cfg != source) | (head != core))
                def _(source=source, core=core, pair=pair):
                    returning(source, core, pair).wait_recv()

    def summed_pairs(source):
        cores = []
        for core in range(2):
            parts = [arecv[source, core, pair].astype(jnp.float32) for pair in range(6)]
            cores.append(((parts[0] + parts[1]) + (parts[2] + parts[3])) + (parts[4] + parts[5]))
        return cores[0] + cores[1]

    conditional = summed_pairs(0)
    unconditional = summed_pairs(1)
    part[...] = unconditional + guide_scale * (conditional - unconditional)
    own_part = pltpu.make_async_copy(part, out_ref, part_sem)
    own_part.start()

    own_part.wait()


def joint(queries, keys, values, w_out, latents, block_mask, lengths, step_index):
    rows, cols = queries.shape[1:]
    hbm = pl.BlockSpec(memory_space=pltpu.HBM)
    dma = pltpu.SemaphoreType.DMA
    regular = pltpu.SemaphoreType.REGULAR
    width = latents.shape[1]
    latent = w_out.shape[1]
    small = jnp.int32
    guided = pl.pallas_call(
        joint_kernel,
        out_shape=jax.ShapeDtypeStruct((width, rows), jnp.float32),
        in_specs=[hbm] * 6,
        out_specs=pl.BlockSpec(memory_space=pl.ANY),
        scratch_shapes=[
            pltpu.VMEM((8 * rows, PAIR), jnp.bfloat16),
            pltpu.VMEM((8 * rows, PAIR), jnp.bfloat16),
            pltpu.VMEM((8 * rows, PAIR), jnp.bfloat16),
            pltpu.VMEM((8, latent, rows), RETURN),
            pltpu.VMEM((2, 2, 6, width, rows), RETURN),
            pltpu.VMEM((latent, cols), jnp.bfloat16),
            pltpu.VMEM((8, 1, 8 * rows), jnp.float32),
            pltpu.VMEM((width, rows), jnp.float32),
            dma((3, 6)),
            dma((3, 8)),
            dma((3,)),
            dma,
            dma((2, 2, 8)),
            dma((2, 2, 6)),
            regular((8,)),
            regular,
            regular,
            dma,
            pltpu.SMEM(block_mask.shape, small),
            pltpu.SMEM(lengths.shape, small),
            dma((2,)),
        ],
        compiler_params=pltpu.CompilerParams(collective_id=0, has_side_effects=True, vmem_limit_bytes=6 * 1024 * 1024),
    )(*[pltpu.with_memory_space_constraint(x, pltpu.HBM) for x in (queries[0], keys[0], values[0], w_out.T, block_mask, lengths)])
    tokens = latents.T
    coef_a, coef_b, coef_a2, coef_b2 = plan(jnp.where(guided == guided, step_index[0], 0))
    denoised = coef_a * tokens - coef_b * guided
    stepped = coef_a2 * denoised + coef_b2 * (coef_b * tokens + coef_a * guided)
    return (denoised.T, stepped.T)


def solution(mesh):
    in_specs = (
        P("cfg", "seq", "head"),
        P("cfg", "seq", "head"),
        P("cfg", "seq", "head"),
        P("head", None),
        P("seq", "cfg"),
        P(),
        P(),
        P(),
    )
    out_specs = (P("seq", "cfg"), P("seq", "cfg"))
    sizes = mesh.shape
    fits = sizes["cfg"] == 2 and sizes["seq"] == 8 and sizes["head"] == 2
    body = joint if fits else local
    return jax.shard_map(body, mesh=mesh, in_specs=in_specs, out_specs=out_specs, check_vma=False)
```

```python
import jax
import jax.numpy as jnp
from jax import lax
from jax.experimental import pallas as pl
from jax.experimental.pallas import tpu as pltpu
from jax.sharding import PartitionSpec as P

HEAD_DIM = 64
STEPS = 50


guide_scale = 6.0
score_scale = 0.125


def from_partner(value, axis, distance):
    mask = 2**distance
    pairs = [(source, source ^ mask) for source in range(lax.axis_size(axis))]
    return lax.ppermute(value, axis, pairs)


def shifted(block, axis, distance):
    devices = range(lax.axis_size(axis))
    route = [((i - distance) % len(devices), i) for i in devices]
    return lax.ppermute(block, axis, route)


def plan(step_value):
    step_float = step_value.astype(jnp.float32)
    first = (STEPS - step_float + 1.0) / (STEPS + 1.0)
    second = (STEPS - step_float) / (STEPS + 1.0)
    abar_now = jnp.exp(-6.0 * first * first)
    abar_next = jnp.exp(-6.0 * second * second)
    return (
        jnp.sqrt(abar_now),
        jnp.sqrt(1.0 - abar_now),
        jnp.sqrt(abar_next),
        jnp.sqrt(1.0 - abar_next),
    )


def regroup_heads(triple, bit, own_shard):
    upper = jnp.right_shift(own_shard, bit) % 2 == 1
    kept = []
    sent = []
    for member in triple:
        width = member.shape[1] // 2
        lower_cols = member[:, :width]
        upper_cols = member[:, width:]
        kept.append(jnp.where(upper, upper_cols, lower_cols))
        sent.append(jnp.where(upper, lower_cols, upper_cols))
    arrived = from_partner((sent[0], sent[1], sent[2]), "seq", bit)
    joined = []
    for mine, theirs in zip(kept, arrived):
        joined.append(
            jnp.where(upper, jnp.concatenate([theirs, mine], 0), jnp.concatenate([mine, theirs], 0))
        )
    return (joined[0], joined[1], joined[2])


def regroup_tokens(member, bit, own_shard):
    upper = jnp.right_shift(own_shard, bit) % 2 == 1
    height = member.shape[0] // 2
    lower_rows = member[:height]
    upper_rows = member[height:]
    kept = jnp.where(upper, upper_rows, lower_rows)
    sent = jnp.where(upper, lower_rows, upper_rows)
    arrived = from_partner(sent, "seq", bit)
    return jnp.where(
        upper, jnp.concatenate([arrived, kept], 1), jnp.concatenate([kept, arrived], 1)
    )


def local(queries, keys, values, w_out, latents, block_mask, lengths, step_index):
    row_count, columns = queries[0].shape
    shard_total = lax.axis_size("seq")
    levels = 1
    group = 2**levels
    own_shard = lax.axis_index("seq")
    triple = (queries[0], keys[0], values[0])
    bit = 0
    triple = regroup_heads(triple, bit, own_shard)
    query_group, key_group, value_group = triple
    group_rows = group * row_count
    group_cols = columns // group
    head_count = group_cols // HEAD_DIM
    group_index = own_shard // group
    group_count = shard_total // group
    query_heads = query_group.reshape(group_rows, head_count, HEAD_DIM)
    slot_offsets = jnp.arange(row_count)
    initial = (
        jnp.full((head_count, group_rows), -1e30, jnp.float32),
        jnp.zeros((head_count, group_rows), jnp.float32),
        jnp.zeros((head_count, group_rows, HEAD_DIM), jnp.float32),
    )

    def absorb(carry, piece, owner):
        key_piece, value_piece = piece
        submask = lax.dynamic_slice(
            block_mask, (group_index * group, owner * group), (group, group)
        )
        live_counts = lax.dynamic_slice_in_dim(lengths, owner * group, group)
        key_valid = (slot_offsets[None, :] < live_counts[:, None]).reshape(group_rows)
        pair_mask = jnp.repeat(jnp.repeat(submask > 0, row_count, axis=0), row_count, axis=1)
        keep = pair_mask & key_valid[None, :]

        def attend(state):
            running, total, accum = state
            scores = (
                jnp.einsum(
                    "qhd,khd->hqk",
                    query_heads,
                    key_piece.reshape(group_rows, head_count, HEAD_DIM),
                    preferred_element_type=jnp.float32,
                )
                * score_scale
            )
            scores = jnp.where(keep[None], scores, -1e30)
            newmax = jnp.maximum(running, jnp.max(scores, axis=-1))
            weights = jnp.where(keep[None], jnp.exp(scores - newmax[..., None]), 0.0)
            factor = jnp.exp(running - newmax)
            total = total * factor + jnp.sum(weights, axis=-1)
            accum = accum * factor[..., None] + jnp.einsum(
                "hqk,khd->hqd",
                weights.astype(jnp.bfloat16),
                value_piece.reshape(group_rows, head_count, HEAD_DIM),
                preferred_element_type=jnp.float32,
            )
            return (newmax, total, accum)

        return lax.cond(jnp.any(submask > 0), attend, lambda state: state, carry)

    carry = absorb(initial, (key_group, value_group), group_index)

    def one_turn(turn_index, state):
        held, totals = state
        held = shifted((held[0], held[1]), "seq", group)
        owner_index = (group_index - turn_index) % group_count
        totals = absorb(totals, held, owner_index)
        return (held, totals)

    held_last, carry = lax.fori_loop(1, group_count, one_turn, ((key_group, value_group), carry))
    running, total, accum = carry
    attended = (
        jnp.transpose(accum / total[..., None], (1, 0, 2))
        .reshape(group_rows, group_cols)
        .astype(jnp.bfloat16)
    )
    for bit in reversed(range(levels)):
        attended = regroup_tokens(attended, bit, own_shard)
    partial_value = jnp.dot(attended, w_out, preferred_element_type=jnp.float32)
    half_index = lax.axis_index("cfg")
    own_width = latents.shape[1]
    own_start = half_index * own_width
    prediction = lax.psum(partial_value, "head")
    mine = lax.dynamic_slice_in_dim(prediction, own_start, own_width, 1)
    outgoing = lax.dynamic_slice_in_dim(prediction, (1 - half_index) * own_width, own_width, 1)
    other_half = from_partner(outgoing, "cfg", 0)
    conditional = jnp.where(half_index == 0, mine, other_half)
    unconditional = jnp.where(half_index == 0, other_half, mine)
    guided = unconditional + guide_scale * (conditional - unconditional)
    coef_a, coef_b, coef_a2, coef_b2 = plan(step_index[0])
    denoised = coef_a * latents - coef_b * guided
    stepped = coef_a2 * denoised + coef_b2 * (coef_b * latents + coef_a * guided)
    return (denoised, stepped)


PAIR = 2 * HEAD_DIM
NEG = -1e30
LOG2E = 1.4426950408889634
ORDER = (4, 0, 1, 2, 3, 5)
RETURN = jnp.bfloat16
SPLIT = 256


def owner_of(pair, head):
    if pair < 4:
        return pair + 2
    return head if pair == 4 else 1 + 5 * head


def joint_kernel(
    q_hbm, k_hbm, v_hbm, w_hbm, mask_hbm, len_hbm,
    out_ref,
    qbuf, kbuf, vbuf, abuf, arecv, wbuf, bias, part,
    send_sem, recv_sem, own_sem, w_sem, ret_send, ret_recv,
    here, cross_ready, pair_ready,
    part_sem, mask_ref, len_ref, small_sem,
):
    cfg = lax.axis_index("cfg")
    me = lax.axis_index("seq")
    head = lax.axis_index("head")
    rows = q_hbm.shape[0]
    half = me // 4
    mesh = pl.DeviceIdType.MESH
    sources = (k_hbm, v_hbm, q_hbm)
    buffers = (kbuf, vbuf, qbuf)

    def slot(kind, shard):
        return buffers[kind].at[pl.ds(pl.multiple_of(shard * rows, 16), rows)]

    def columns(kind, pair):
        return sources[kind].at[:, pl.ds(pl.multiple_of(pair * PAIR, PAIR), PAIR)]

    def remote(kind, pair, target):
        return pltpu.make_async_remote_copy(
            src_ref=columns(kind, pair),
            dst_ref=slot(kind, me),
            send_sem=send_sem.at[kind, pair],
            recv_sem=recv_sem.at[kind, me],
            device_id={"seq": target},
            device_id_type=mesh,
        )

    def arrival(kind, shard):
        return pltpu.make_async_remote_copy(
            src_ref=slot(kind, shard),
            dst_ref=slot(kind, shard),
            send_sem=send_sem.at[kind, 0],
            recv_sem=recv_sem.at[kind, shard],
            device_id={"seq": shard},
            device_id_type=mesh,
        )

    def own_copy(kind, pair):
        return pltpu.make_async_copy(columns(kind, pair), slot(kind, me), own_sem.at[kind])

    width = part.shape[0]

    def channels(half_index):
        return pl.ds(pl.multiple_of(half_index * width, 16), width)

    def returned(target, core, pair, shard, index):
        return pltpu.make_async_remote_copy(
            src_ref=abuf.at[index, channels(target)],
            dst_ref=arecv.at[cfg, head, pair],
            send_sem=ret_send.at[target, core, index],
            recv_sem=ret_recv.at[cfg, head, pair],
            device_id={"cfg": target, "seq": shard, "head": core},
            device_id_type=mesh,
        )

    def returning(source, core, pair):
        return pltpu.make_async_remote_copy(
            src_ref=arecv.at[source, core, pair],
            dst_ref=arecv.at[source, core, pair],
            send_sem=ret_send.at[0, 0, 0],
            recv_sem=ret_recv.at[source, core, pair],
            device_id={"cfg": 1 - cfg},
            device_id_type=mesh,
        )

    inner = (me >= 2) & (me < 6)
    low = me == head
    high = me == owner_of(5, head)
    active = inner | low | high
    my_pair = jnp.where(inner, me - 2, jnp.where(low, 4, 5))

    barrier = pltpu.get_barrier_semaphore()
    for other in range(1, 8):

        @pl.when(other > me)
        def _(other=other):
            pl.semaphore_signal(barrier, inc=1, device_id={"seq": other}, device_id_type=mesh)

    @pl.when(head == 0)
    def _():
        pl.semaphore_signal(barrier, inc=1, device_id={"head": 1}, device_id_type=mesh)

    w_copy = pltpu.make_async_copy(w_hbm, wbuf, w_sem)
    small_copies = [
        pltpu.make_async_copy(mask_hbm, mask_ref, small_sem.at[0]),
        pltpu.make_async_copy(len_hbm, len_ref, small_sem.at[1]),
    ]

    greeted = me + cfg + head

    @pl.when(greeted > 0)
    def _():
        pl.semaphore_wait(barrier, greeted)

    @pl.when(cfg == 0)
    def _():
        pl.semaphore_signal(barrier, inc=1, device_id={"cfg": 1}, device_id_type=mesh)

    for other in range(7):

        @pl.when(other < me)
        def _(other=other):
            pl.semaphore_signal(here.at[me], inc=1, device_id={"seq": other}, device_id_type=mesh)

    def await_shard(shard):
        @pl.when(shard > me)
        def _():
            pl.semaphore_wait(here.at[shard], 1)

    def send(kind, place):
        pair = ORDER[place]
        target = owner_of(pair, head)

        @pl.when(target != me)
        def _():
            remote(kind, pair, target).start()

    await_shard(1)
    send(0, 0)
    send(1, 0)

    @pl.when(head == 0)
    def _():
        send(0, 5)
        send(1, 5)

    for place in range(1, 3):
        await_shard(place + 1)
        send(0, place)
        send(1, place)

    @pl.when(active)
    def _():
        for kind in range(3):
            own_copy(kind, my_pair).start()

    for copy in small_copies:
        copy.start()
    w_copy.start()

    @pl.when(me >= 6)
    def _():
        for place in range(3):
            send(2, place)

        @pl.when(head == 0)
        def _():
            send(2, 5)

    for place in range(3, 5):
        await_shard(place + 1)
        send(0, place)
        send(1, place)

        @pl.when(me == 0)
        def _(place=place):
            send(2, place)

    await_shard(6)

    @pl.when(jnp.logical_not(head == 0))
    def _():
        send(0, 5)
        send(1, 5)

    @pl.when(me < 6)
    def _():
        for place in range(3):
            send(2, place)

    @pl.when(me > 0)
    def _():
        for place in range(3, 5):
            send(2, place)

    @pl.when((me < 6) | (head == 1))
    def _():
        send(2, 5)

    await_shard(7)

    for ready, place, axis in ((pair_ready, head, "head"), (cross_ready, cfg, "cfg")):

        @pl.when(place == 1)
        def _(ready=ready, axis=axis):
            pl.semaphore_signal(ready, inc=1, device_id={axis: 0}, device_id_type=mesh)

        pl.semaphore_wait(ready, 1)

        @pl.when(place == 0)
        def _(ready=ready, axis=axis):
            pl.semaphore_signal(ready, inc=1, device_id={axis: 1}, device_id_type=mesh)


    for copy in small_copies:
        copy.wait()
    @pl.when(active)
    def _():
        lane = lax.broadcasted_iota(jnp.int32, (8, 8 * rows), 1)
        row_shard = lax.broadcasted_iota(jnp.int32, (8, 8 * rows), 0)
        position = lane % rows
        limit = jnp.zeros((8, 8 * rows), jnp.int32)
        for j in range(8):
            column = jnp.zeros((8, 8 * rows), jnp.int32)
            for i in range(8):
                live = jnp.where(mask_ref[i, j] > 0, len_ref[j], 0)
                column = jnp.where(row_shard == i, live, column)
            limit = jnp.where((lane >= j * rows) & (lane < (j + 1) * rows), column, limit)
        bias[...] = jnp.where(position < limit, 0.0, NEG).reshape(8, 1, 8 * rows)

        w_copy.wait()
        weight = wbuf[:, pl.ds(pl.multiple_of(my_pair * PAIR, PAIR), PAIR)]

        for kind in range(2):
            own_copy(kind, my_pair).wait()
        own_copy(2, my_pair).wait()

        def await_tokens(shards):
            for kind in range(2):
                for shard in shards:

                    @pl.when(shard != me)
                    def _(kind=kind, shard=shard):
                        arrival(kind, shard).wait_recv()

        def stack(first, count):
            height = count * rows
            query = qbuf[pl.ds(pl.multiple_of(first * rows, 16), height)]
            zero = jnp.zeros_like(query)
            left = lax.broadcasted_iota(jnp.int32, (height, PAIR), 1) < HEAD_DIM
            both = [jnp.where(left, query, zero), jnp.where(left, zero, query)]
            return jnp.concatenate(both, axis=0), left

        def scored(stacked, first, count, start, stop):
            scores = lax.dot_general(
                stacked,
                kbuf[start:stop],
                (((1,), (1,)), ((), ())),
                preferred_element_type=jnp.float32,
            )
            shape = scores.shape
            limits = bias[pl.ds(first, count), :, start:stop][None]
            scores = scores.reshape(2, count, rows, stop - start) + limits
            return scores.reshape(shape)

        def weighed(scores, top, start, stop):
            weights = jnp.exp2((scores - top) * (score_scale * LOG2E))
            total = jnp.sum(weights, axis=1, keepdims=True)
            summed = jnp.dot(
                weights.astype(jnp.bfloat16), vbuf[start:stop], preferred_element_type=jnp.float32
            )
            return total, summed

        def project(first, count, left, total, summed):
            height = count * rows
            summed = summed / total
            attended = jnp.where(left, summed[:height], summed[height:]).astype(jnp.bfloat16)
            for index in range(count):
                abuf[first + index] = lax.dot_general(
                    weight,
                    attended[index * rows : (index + 1) * rows],
                    (((1,), (1,)), ((), ())),
                    preferred_element_type=jnp.float32,
                ).astype(RETURN)

        def attend(first, count):
            stacked, left = stack(first, count)
            scores = scored(stacked, first, count, 0, 8 * rows)
            top = jnp.max(scores, axis=1, keepdims=True)
            project(first, count, left, *weighed(scores, top, 0, 8 * rows))

        def give(shard):
            for target in range(2):
                for core in range(2):
                    @pl.when((shard != me) | (target != cfg) | (core != head))
                    def _(target=target, core=core):
                        returned(target, core, my_pair, shard, shard).start()

        def await_query(shard):
            @pl.when(shard != me)
            def _():
                arrival(2, shard).wait_recv()

        def batch(first, count):
            for shard in [first + index for index in range(count)]:
                await_query(shard)
            attend(first, count)
            for shard in [first + index for index in range(count)]:
                give(shard)

        @pl.when(half == 0)
        def _():
            await_tokens(range(4))
            for shard in range(4):
                await_query(shard)
            stacked, left = stack(0, 4)
            near = scored(stacked, 0, 4, 0, SPLIT)
            near_top = jnp.max(near, axis=1, keepdims=True)
            near_total, near_summed = weighed(near, near_top, 0, SPLIT)
            await_tokens(range(4, 8))
            stop = 8 * rows
            far = scored(stacked, 0, 4, SPLIT, stop)
            top = jnp.maximum(near_top, jnp.max(far, axis=1, keepdims=True))
            total, summed = weighed(far, top, SPLIT, stop)
            scale = jnp.exp2((near_top - top) * (score_scale * LOG2E))
            project(0, 4, left, total + near_total * scale, summed + near_summed * scale)
            for shard in range(4):
                give(shard)

        @pl.when(half == 1)
        def _():
            await_tokens(range(8))

        def turn(index, carry):
            batch(jnp.where(index == 0, 0, jnp.where(index == 3, 2, 8 - 2 * index)), 2)
            return carry

        lax.fori_loop(1 - half, 3 + half, turn, 0)

        arecv[cfg, head, my_pair] = abuf[me, channels(cfg)]

    @pl.when(jnp.logical_not(active))
    def _():
        w_copy.wait()

    for kind in range(3):
        for place in range(6):
            pair = ORDER[place]
            target = owner_of(pair, head)

            @pl.when(target != me)
            def _(kind=kind, pair=pair, target=target):
                remote(kind, pair, target).wait_send()

    @pl.when(active)
    def _():
        for target in range(2):
            for core in range(2):
                for shard in range(8):

                    @pl.when((shard != me) | (target != cfg) | (core != head))
                    def _(target=target, core=core, shard=shard):
                        returned(target, core, my_pair, shard, shard).wait_send()

    for source in range(2):
        for core in range(2):
            for pair in range(6):

                @pl.when((owner_of(pair, core) != me) | (cfg != source) | (head != core))
                def _(source=source, core=core, pair=pair):
                    returning(source, core, pair).wait_recv()

    def summed_pairs(source):
        cores = []
        for core in range(2):
            parts = [arecv[source, core, pair].astype(jnp.float32) for pair in range(6)]
            cores.append(((parts[0] + parts[1]) + (parts[2] + parts[3])) + (parts[4] + parts[5]))
        return cores[0] + cores[1]

    conditional = summed_pairs(0)
    unconditional = summed_pairs(1)
    part[...] = unconditional + guide_scale * (conditional - unconditional)
    own_part = pltpu.make_async_copy(part, out_ref, part_sem)
    own_part.start()

    own_part.wait()


def joint(queries, keys, values, w_out, latents, block_mask, lengths, step_index):
    rows, cols = queries.shape[1:]
    hbm = pl.BlockSpec(memory_space=pltpu.HBM)
    dma = pltpu.SemaphoreType.DMA
    regular = pltpu.SemaphoreType.REGULAR
    width = latents.shape[1]
    latent = w_out.shape[1]
    small = jnp.int32
    guided = pl.pallas_call(
        joint_kernel,
        out_shape=jax.ShapeDtypeStruct((width, rows), jnp.float32),
        in_specs=[hbm] * 6,
        out_specs=pl.BlockSpec(memory_space=pl.ANY),
        scratch_shapes=[
            pltpu.VMEM((8 * rows, PAIR), jnp.bfloat16),
            pltpu.VMEM((8 * rows, PAIR), jnp.bfloat16),
            pltpu.VMEM((8 * rows, PAIR), jnp.bfloat16),
            pltpu.VMEM((8, latent, rows), RETURN),
            pltpu.VMEM((2, 2, 6, width, rows), RETURN),
            pltpu.VMEM((latent, cols), jnp.bfloat16),
            pltpu.VMEM((8, 1, 8 * rows), jnp.float32),
            pltpu.VMEM((width, rows), jnp.float32),
            dma((3, 6)),
            dma((3, 8)),
            dma((3,)),
            dma,
            dma((2, 2, 8)),
            dma((2, 2, 6)),
            regular((8,)),
            regular,
            regular,
            dma,
            pltpu.SMEM(block_mask.shape, small),
            pltpu.SMEM(lengths.shape, small),
            dma((2,)),
        ],
        compiler_params=pltpu.CompilerParams(collective_id=0, has_side_effects=True, vmem_limit_bytes=6 * 1024 * 1024),
    )(*[pltpu.with_memory_space_constraint(x, pltpu.HBM) for x in (queries[0], keys[0], values[0], w_out.T, block_mask, lengths)])
    tokens = latents.T
    coef_a, coef_b, coef_a2, coef_b2 = plan(jnp.where(guided == guided, step_index[0], 0))
    denoised = coef_a * tokens - coef_b * guided
    stepped = coef_a2 * denoised + coef_b2 * (coef_b * tokens + coef_a * guided)
    return (denoised.T, stepped.T)


def solution(mesh):
    in_specs = (
        P("cfg", "seq", "head"),
        P("cfg", "seq", "head"),
        P("cfg", "seq", "head"),
        P("head", None),
        P("seq", "cfg"),
        P(),
        P(),
        P(),
    )
    out_specs = (P("seq", "cfg"), P("seq", "cfg"))
    sizes = mesh.shape
    fits = sizes["cfg"] == 2 and sizes["seq"] == 8 and sizes["head"] == 2
    body = joint if fits else local
    return jax.shard_map(body, mesh=mesh, in_specs=in_specs, out_specs=out_specs, check_vma=False)
```
